32 devices in a mesh: row: 4 (over z), col: 8 (over y, x, core).
Axes of the slice: x: 2, y: 2, z: 4, core: 2. Of those that a mesh axis runs over, the one named last changes fastest.
Arguments:
- strain: bfloat16 [256, 33280], P(('row', 'col')), may hold values from -6 to 6
- file_channels: int32 [256], P(('row', 'col')), may hold values from 0 to 127, as said below
- file_counts: int32 [32], P(('row', 'col')), may hold values from 0 to 8, as said below
- window_start: int32 [32], P(('row', 'col')), may hold values from 0 to 512
Outputs:
- correlations: bfloat16 [128, 128, 1024], P('row', 'col')
The draws below stay inside these ranges and needn't reach their ends.
Inputs may be any that keep to these rules, and one draw needn't show every extreme that they name: `file_channels`: the first file_counts[d] slots of file d are live. The live slots of the 4 files with one col index hold, each exactly once, the channels g whose owner ((g // 4) // 8, (g // 4) % 8) has that col index; dead slots hold arbitrary channel numbers. One file holds at most 2 channels of one owner, and exactly 2 for some file and owner in every group of files with one col index. `file_counts`: in every group of files with one col index some file has all 8 slots live.
All inputs are finite; a program needn't handle non-finite values.
Results may differ from the reference program's by a relative error of at most 0.0076.
Values may be sent and summed in bfloat16 or wider, within the bound.
A program may use at most 128 MiB of HBM per device.

```python
import math
import jax
import jax.numpy as jnp
from jax import lax

NF = 2048
NT = 4096
LAGS = 1024
SEGS = 8
CH_DEV = 4
CAP = 2
SPAN = 512
SMOOTH = 32
EDGE = 128
SLOTS = 8
NCH = 128
TFILE = 33280
N_ROW = 4
N_COL = 8
DEVICES = 32


def file_layout(key):
    layout_key = jax.random.fold_in(key, 11)
    column_keys = jax.random.split(layout_key, N_COL)

    def one_column(column_key, column):
        sub_keys = jax.random.split(column_key, 5)
        file_order = jax.random.permutation(sub_keys[0], N_ROW)
        offsets = jax.random.randint(sub_keys[2], (N_ROW,), 0, N_ROW - 1)
        owners = jnp.repeat(jnp.arange(N_ROW, dtype=jnp.int32), CH_DEV)
        within = jnp.tile(jnp.arange(CH_DEV, dtype=jnp.int32), N_ROW)
        hot_pair = within < CAP
        spread = within - CAP
        position = jnp.where(hot_pair, 0, 1 + jnp.mod(offsets[owners] + spread, N_ROW - 1))
        file_of = file_order[position].astype(jnp.int32)
        channels = ((owners * N_COL + column) * CH_DEV + within).astype(jnp.int32)
        item_count = N_ROW * CH_DEV
        ranking = jax.random.permutation(sub_keys[3], item_count).astype(jnp.int32)
        sorted_index = jnp.argsort(file_of * item_count + ranking, stable=True)
        sorted_files = file_of[sorted_index]
        counts = jnp.sum((file_of[None, :] == jnp.arange(N_ROW, dtype=jnp.int32)[:, None]).astype(jnp.int32), axis=1)
        starts = jnp.cumsum(counts) - counts
        slot_of = jnp.arange(item_count, dtype=jnp.int32) - starts[sorted_files]
        filler = jax.random.randint(sub_keys[4], (N_ROW, SLOTS), 0, NCH)
        slot_table = filler.at[sorted_files, slot_of].set(channels[sorted_index])
        return (slot_table.astype(jnp.int32), counts.astype(jnp.int32))
    tables, counts = jax.vmap(one_column)(column_keys, jnp.arange(N_COL, dtype=jnp.int32))
    return (jnp.transpose(tables, (1, 0, 2)).reshape(-1), jnp.transpose(counts).reshape(-1))


def draw_file_channels(key, part):
    return file_layout(key)[0]


def draw_file_counts(key, part):
    return file_layout(key)[1]


def touch_ends(drawn, own_key, least, high):
    place = [jax.random.randint(jax.random.fold_in(own_key, axis), (), 0, length) for axis, length in enumerate(drawn.shape)]
    main_axis = drawn.shape.index(max(drawn.shape))
    neighbour = place[:main_axis] + [(place[main_axis] + 1) % drawn.shape[main_axis]] + place[main_axis + 1:]
    return drawn.at[tuple(place)].set(least).at[tuple(neighbour)].set(high)


def level_of(key, dims, pieces, smallest, largest):
    loudness, own = 1.0, jax.random.fold_in(key, 6)
    for dim, shards_of in pieces:
        draws = jnp.exp(jax.random.uniform(jax.random.fold_in(own, dim), (shards_of,), jnp.float32, smallest / len(pieces), largest / len(pieces)))
        loudness = loudness * jnp.repeat(draws, dims[dim] // shards_of).reshape([-1 if axis == dim else 1 for axis in range(len(dims))])
    return loudness


def bell_draw(key, shape, scale, bound, shards=(), kind=jnp.bfloat16):
    values = jax.random.normal(key, shape, jnp.float32) * scale
    if len(shards) > 0:
        values = level_of(key, shape, shards, -0.22, 0.18) * values
    return jnp.clip(values, min=-bound, max=bound).astype(kind)


def setup_inputs(seed: int = 0) -> dict:
    key_list = jax.random.split(jax.random.key(seed), 5)
    strain = bell_draw(key_list[0], (DEVICES * SLOTS, TFILE), 1.0, 6.0, ((0, 32),))
    file_channels = draw_file_channels(jax.random.fold_in(key_list[4], 71), 0)
    file_counts = draw_file_counts(jax.random.fold_in(key_list[4], 71), 0)
    window_start = touch_ends(jax.random.randint(key_list[3], (DEVICES,), 0, SPAN + 1), jax.random.fold_in(key_list[3], 1), 0, SPAN).astype(jnp.int32)
    return {"strain": strain, "file_channels": file_channels, "file_counts": file_counts, "window_start": window_start}


def dft_block(first_freq, freq_count, length):
    sample_index = jnp.arange(length, dtype=jnp.int32)[:, None]
    freq_index = first_freq + jnp.arange(freq_count, dtype=jnp.int32)[None, :]
    phases = jnp.mod(sample_index * freq_index, length).astype(jnp.float32) * (2.0 * math.pi / length)
    return jnp.concatenate([jnp.cos(phases), -jnp.sin(phases)], axis=1).astype(jnp.bfloat16)

def lag_table():
    freq_index = jnp.arange(NF, dtype=jnp.int32)[:, None]
    lag_index = jnp.arange(LAGS, dtype=jnp.int32)[None, :] - LAGS // 2
    phases = jnp.mod(freq_index * lag_index, NT).astype(jnp.float32) * (2.0 * math.pi / NT)
    return jnp.concatenate([jnp.cos(phases), -jnp.sin(phases)], axis=0).astype(jnp.bfloat16)

def band_taper(freq_count):
    freq_index = jnp.arange(freq_count, dtype=jnp.float32)
    distance = jnp.minimum(freq_index + 0.5, freq_count - freq_index - 0.5)
    rising = jnp.minimum(distance / EDGE, 1.0)
    return jnp.sin(0.5 * math.pi * rising) ** 2

def whiten(real_part, imag_part):
    powers = real_part * real_part + imag_part * imag_part
    padded = jnp.pad(powers, ((0, 0), (SMOOTH + 1, SMOOTH)))
    running = jnp.cumsum(padded, axis=1)
    window_sum = running[:, 2 * SMOOTH + 1:] - running[:, :powers.shape[1]]
    scaling = band_taper(powers.shape[1])[None, :] / jnp.sqrt(window_sum / (2 * SMOOTH + 1) + 1e-06)
    return (real_part * scaling, imag_part * scaling)

def reference(strain, file_channels, file_counts, window_start):
    file_total = file_counts.shape[0]
    file_blocks = strain.reshape(file_total, SLOTS, strain.shape[1])

    def cut_window(block, first_sample):
        return lax.dynamic_slice_in_dim(block, first_sample, SEGS * NT, 1)
    windows = jax.vmap(cut_window)(file_blocks, window_start).reshape(file_total * SLOTS, SEGS * NT)
    live_slot = (jnp.arange(SLOTS, dtype=jnp.int32)[None, :] < file_counts[:, None]).reshape(-1)
    target = jnp.where(live_slot, file_channels, NCH).astype(jnp.int32)
    traces = jnp.zeros((NCH + 1, SEGS * NT), jnp.bfloat16).at[target].set(windows)[:NCH]
    segment_rows = traces.reshape(NCH * SEGS, NT).astype(jnp.float32)
    table = dft_block(jnp.int32(0), NF, NT).astype(jnp.float32)
    product = jnp.dot(segment_rows, table, precision=lax.Precision.HIGHEST)
    real_part, imag_part = whiten(product[:, :NF], product[:, NF:])
    spectra = jnp.stack([real_part.reshape(NCH, SEGS, NF), imag_part.reshape(NCH, SEGS, NF)], axis=1).astype(jnp.bfloat16)
    spectra = lax.optimization_barrier(spectra).astype(jnp.float32)
    column = jnp.arange(NCH, dtype=jnp.int32)
    group_size = N_ROW * CH_DEV
    col_ids = (column % group_size // CH_DEV * N_COL + column // group_size) * CH_DEV + column % CH_DEV
    col_spectra = spectra[col_ids]
    flipped = jnp.concatenate([-col_spectra[:, 1:2], col_spectra[:, 0:1]], axis=1)
    inverse = lag_table().astype(jnp.float32)
    norm_scale = 1.0 / math.sqrt(SEGS * NF)

    def one_block(block_index):
        first_row = block_index * 8
        row_block = lax.dynamic_slice_in_dim(spectra, first_row, 8, 0)
        real_cross = jnp.einsum('icsf,jcsf->ijf', row_block, col_spectra, precision=lax.Precision.HIGHEST)
        imag_cross = jnp.einsum('icsf,jcsf->ijf', row_block, flipped, precision=lax.Precision.HIGHEST)
        cross = jnp.concatenate([real_cross, imag_cross], axis=2).astype(jnp.bfloat16)
        cross = lax.optimization_barrier(cross).astype(jnp.float32)
        lagged = jnp.dot(cross.reshape(8 * NCH, 2 * NF), inverse, precision=lax.Precision.HIGHEST).reshape(8, NCH, LAGS)
        row_ids = first_row + jnp.arange(8, dtype=jnp.int32)
        keep_pair = (row_ids[:, None] != col_ids[None, :]).astype(jnp.float32)
        return (lagged * (keep_pair[:, :, None] * norm_scale)).astype(jnp.bfloat16)
    blocks_out = lax.map(one_block, jnp.arange(NCH // 8, dtype=jnp.int32))
    return blocks_out.reshape(NCH, NCH, LAGS)
```

```python
import functools
import math

import jax
import jax.numpy as jnp
import numpy as np
from jax import lax
from jax.experimental import pallas as pl
from jax.experimental.pallas import tpu as pltpu
from jax.sharding import PartitionSpec as P

NF = 2048
NT = 4096
LAGS = 1024
SEGS = 8
CH_DEV = 4
CAP = 2
SMOOTH = 32
EDGE = 128
N1 = 16
N2 = NT // N1
F2 = NF // N1
HALF = LAGS // 2
PAIR = 2 * F2
STEPS = NF // PAIR
TILE = 256
TILES = 2 * HALF // TILE


def forward_tables():
    n2 = np.arange(N2)
    f1 = np.arange(N1)
    f2 = np.arange(F2)
    angle = 2 * np.pi * (np.outer(f1, n2) % NT) / NT
    twiddle = np.stack([np.cos(angle), -np.sin(angle)]).astype(np.float32)
    angle = 2 * np.pi * (np.outer(n2, f2) % N2) / N2
    c, s = np.cos(angle), np.sin(angle)
    second = np.block([[c, -s], [s, c]]).astype(np.float32)
    high = second.astype(jnp.bfloat16)
    low = (second - high.astype(np.float32)).astype(jnp.bfloat16)
    f = f1[:, None] + N1 * f2[None, :]
    distance = np.minimum(f + 0.5, NF - f - 0.5)
    taper = np.sin(0.5 * np.pi * np.minimum(distance / EDGE, 1.0)) ** 2
    turn = np.pi * f / NT
    shape = np.stack([taper, np.cos(turn), -np.sin(turn)]).astype(np.float32)
    return twiddle, high, low, shape


def lag_tables():
    m2 = 2 * np.arange(HALF) + 1
    f1 = np.arange(N1)
    f2 = N1 * np.arange(F2)
    a = np.pi * (np.outer(f1, m2) % (2 * NT)) / NT
    b = np.pi * (np.outer(f2, m2) % (2 * NT)) / NT
    ac, as_, bc, bs = [jnp.asarray(t, jnp.float32) for t in (np.cos(a), np.sin(a), np.cos(b), np.sin(b))]
    c = ac[:, None] * bc[None] - as_[:, None] * bs[None]
    s = -(as_[:, None] * bc[None] + ac[:, None] * bs[None])
    c = c.reshape(STEPS, PAIR, HALF).astype(jnp.bfloat16)
    s = s.reshape(STEPS, PAIR, HALF).astype(jnp.bfloat16)
    parts = [t[:, :, k : k + TILE] for t in (c, s) for k in range(0, HALF, TILE)]
    return jnp.stack(parts, axis=1)


def shifted(value, lanes, amount):
    rolled = pltpu.roll(value, amount % F2, 1)
    source = lanes - amount
    return jnp.where((source >= 0) & (source < F2), rolled, 0.0)


def spectra_kernel(x_ref, tw_ref, hi_ref, lo_ref, shape_ref, row_ref, col_ref, z_ref):
    rows = x_ref.shape[0]
    cosines = np.cos(2 * np.pi * np.arange(N1) / N1)
    sines = np.sin(2 * np.pi * np.arange(N1) / N1)

    def combine(values, weights):
        total = None
        for v, w in zip(values, weights):
            if abs(w) < 1e-9:
                continue
            term = v if abs(w - 1) < 1e-9 else (-v if abs(w + 1) < 1e-9 else v * np.float32(w))
            total = term if total is None else total + term
        return total

    for h in range(0, N2, 128):
        xs = [x_ref[:, k * N2 + h : k * N2 + h + 128].astype(jnp.float32) for k in range(N1)]
        even = [xs[k] + xs[k + N1 // 2] for k in range(N1 // 2)]
        odd = [xs[k] - xs[k + N1 // 2] for k in range(N1 // 2)]
        for f in range(N1 // 2 + 1):
            src = even if f % 2 == 0 else odd
            re = combine(src, [cosines[f * k % N1] for k in range(N1 // 2)])
            im = combine(src, [-sines[f * k % N1] for k in range(N1 // 2)])
            for f1, sign in {f: 1.0, (N1 - f) % N1: -1.0}.items() if f not in (0, N1 // 2) else ((f, 1.0),):
                tc = tw_ref[0, f1 : f1 + 1, h : h + 128]
                ts = tw_ref[1, f1 : f1 + 1, h : h + 128]
                if im is None:
                    zr, zi = re * tc, re * ts
                else:
                    i = im if sign > 0 else -im
                    zr, zi = re * tc - i * ts, re * ts + i * tc
                z_ref[f1 * rows : (f1 + 1) * rows, h : h + 128] = zr
                z_ref[f1 * rows : (f1 + 1) * rows, N2 + h : N2 + h + 128] = zi
    z = z_ref[...]
    zh = z.astype(jnp.bfloat16)
    zl = (z - zh.astype(jnp.float32)).astype(jnp.bfloat16)
    dot = functools.partial(jnp.dot, preferred_element_type=jnp.float32)
    z_ref[:, : 2 * F2] = dot(zh, hi_ref[...]) + dot(zl, hi_ref[...]) + dot(zh, lo_ref[...])

    lanes = lax.broadcasted_iota(jnp.int32, (rows, F2), 1)
    part = lambda f1, c: z_ref[f1 * rows : (f1 + 1) * rows, c * F2 : (c + 1) * F2]
    power = []
    for f1 in range(N1):
        re, im = part(f1, 0), part(f1, 1)
        power.append(re * re + im * im)
    prefix, suffix = [power[0]], [power[-1]]
    for k in range(1, N1):
        prefix.append(prefix[-1] + power[k])
        suffix.append(suffix[-1] + power[N1 - 1 - k])
    suffix = suffix[::-1]
    total = prefix[-1]
    reach = SMOOTH // N1
    middle = total
    for k in range(1, reach):
        middle = middle + shifted(total, lanes, k) + shifted(total, lanes, -k)
    for f1 in range(N1):
        window = middle + shifted(suffix[f1], lanes, reach) + shifted(prefix[f1], lanes, -reach)
        scale = shape_ref[0, f1 : f1 + 1] * lax.rsqrt(window * (1.0 / (2 * SMOOTH + 1)) + 1e-06)
        re, im = part(f1, 0) * scale, part(f1, 1) * scale
        tc, ts = shape_ref[1, f1 : f1 + 1], shape_ref[2, f1 : f1 + 1]
        tr, ti = re * tc - im * ts, re * ts + im * tc
        for ch in range(rows // SEGS):
            own = slice(ch * SEGS, (ch + 1) * SEGS)
            at = slice(f1 * F2, (f1 + 1) * F2)
            col_ref[ch, :, at] = jnp.concatenate([re[own], im[own]], axis=0).astype(jnp.bfloat16)
            row_ref[ch, :, at] = jnp.concatenate([tr[own], ti[own]], axis=0).astype(jnp.bfloat16)


def spectra_of(segment_rows):
    channels = segment_rows.shape[0] // SEGS
    shape = jax.ShapeDtypeStruct((channels, 2 * SEGS, NF), jnp.bfloat16)
    return pl.pallas_call(
        spectra_kernel,
        out_shape=(shape, shape),
        scratch_shapes=[pltpu.VMEM((N1 * channels * SEGS, 2 * N2), jnp.float32)],
        compiler_params=pltpu.CompilerParams(vmem_limit_bytes=48 << 20),
    )(segment_rows, *[jnp.asarray(t) for t in forward_tables()])


def tree(terms):
    while len(terms) > 1:
        terms = [terms[k] + terms[k + 1] for k in range(0, len(terms), 2)]
    return terms[0]


def correlate_kernel(row_total, col_total, a_ref, b_ref, w_ref, keep_ref, flip_ref, out_ref, a32, cross, acc):
    t = pl.program_id(0)
    share = row_total // TILES
    now = lax.rem(t, 2)
    before = 1 - now

    def cross_rows(first):
        for k in range(share):
            g = first + k
            for h in range(0, PAIR, F2):
                lane = slice(h, h + F2)
                real, imag = [], []
                for s in range(SEGS):
                    ar = jnp.broadcast_to(a32[g, s : s + 1, lane], (col_total, F2)).astype(jnp.bfloat16)
                    ai = jnp.broadcast_to(a32[g, SEGS + s : SEGS + s + 1, lane], (col_total, F2)).astype(jnp.bfloat16)
                    br, bi = b_ref[s, :, lane], b_ref[SEGS + s, :, lane]
                    real.append(ar * br + ai * bi)
                    imag.append(ai * br - ar * bi)
                at = pl.ds(pl.multiple_of(g * col_total, 16), col_total)
                cross[now, 0, at, lane] = tree(real)
                cross[now, 1, at, lane] = tree(imag)

    def lag_tile(i):
        part = jnp.dot(cross[before, i // (TILES // 2)], w_ref[0, i], preferred_element_type=jnp.float32)
        acc[i] = acc[i] + part

    def widen():
        a32[...] = a_ref[...].astype(jnp.float32)

    @pl.when(t == 0)
    def _():
        widen()
        acc[...] = jnp.zeros_like(acc)

        @pl.loop(0, TILES)
        def _(i):
            cross_rows(i * share)

    @pl.when((t > 0) & (t < STEPS))
    def _():
        widen()

        @pl.loop(0, TILES)
        def _(i):
            lag_tile(i)
            cross_rows(i * share)

    @pl.when(t == STEPS)
    def _():
        @pl.loop(0, TILES)
        def _(i):
            lag_tile(i)

        keep = keep_ref[...]
        half = TILES // 2
        for k in range(half):
            up = (acc[k] + acc[half + k]) * keep
            down = (acc[k] - acc[half + k]) * keep
            out_ref[:, HALF + k * TILE : HALF + (k + 1) * TILE] = up.astype(jnp.bfloat16)
            turned = jnp.dot(down.astype(jnp.bfloat16), flip_ref[...], preferred_element_type=jnp.float32)
            out_ref[:, HALF - (k + 1) * TILE : HALF - k * TILE] = turned.astype(jnp.bfloat16)


def correlate(row_spectra, col_spectra, keep, tables):
    row_total = row_spectra.shape[0]
    col_total = col_spectra.shape[1]
    pairs = row_total * col_total
    flip = np.eye(TILE, dtype=np.float32)[::-1]
    step = lambda t: jnp.minimum(t, STEPS - 1)
    fixed = lambda shape: pl.BlockSpec(shape, lambda t: (0,) * len(shape), pipeline_mode=pl.Buffered(1))
    return pl.pallas_call(
        functools.partial(correlate_kernel, row_total, col_total),
        grid=(STEPS + 1,),
        in_specs=[
            pl.BlockSpec((row_total, 2 * SEGS, PAIR), lambda t: (0, 0, step(t))),
            pl.BlockSpec((2 * SEGS, col_total, PAIR), lambda t: (0, 0, step(t))),
            pl.BlockSpec((1, TILES, PAIR, TILE), lambda t: (jnp.maximum(t - 1, 0), 0, 0, 0)),
            fixed((pairs, 1)),
            fixed((TILE, TILE)),
        ],
        out_specs=fixed((pairs, LAGS)),
        out_shape=jax.ShapeDtypeStruct((pairs, LAGS), jnp.bfloat16),
        scratch_shapes=[
            pltpu.VMEM((row_total, 2 * SEGS, PAIR), jnp.float32),
            pltpu.VMEM((2, 2, pairs, PAIR), jnp.bfloat16),
            pltpu.VMEM((TILES, pairs, TILE), jnp.float32),
        ],
        compiler_params=pltpu.CompilerParams(vmem_limit_bytes=56 << 20),
    )(row_spectra, col_spectra, tables, keep, jnp.asarray(flip, jnp.bfloat16))


def local(strain, file_channels, file_counts, window_start):
    row_count = lax.axis_size("row")
    col_count = lax.axis_size("col")
    my_row = lax.axis_index("row")
    my_col = lax.axis_index("col")
    slot_total = strain.shape[0]
    window = lax.dynamic_slice_in_dim(strain, window_start[0], SEGS * NT, 1)
    slot_index = jnp.arange(slot_total, dtype=jnp.int32)
    live_slot = slot_index < file_counts[0]
    owner_row = file_channels // CH_DEV // col_count
    local_slot = file_channels % CH_DEV
    same_owner = (owner_row[:, None] == owner_row[None, :]) & live_slot[None, :]
    earlier = slot_index[None, :] < slot_index[:, None]
    position = jnp.sum((same_owner & earlier).astype(jnp.int32), axis=1)
    target = owner_row * CAP + position
    routing = (
        jnp.arange(row_count * CAP, dtype=jnp.int32)[:, None] == target[None, :]
    ) & live_slot[None, :]
    outgoing = jnp.dot(
        routing.astype(jnp.bfloat16), window, preferred_element_type=jnp.float32
    ).astype(jnp.bfloat16)
    labels = jnp.sum(jnp.where(routing, local_slot[None, :] + 1, 0), axis=1) - 1
    tail = jnp.broadcast_to(labels.astype(jnp.bfloat16)[:, None], (row_count * CAP, 128))
    outgoing = jnp.concatenate([outgoing, tail], axis=1)
    arrived = lax.all_to_all(
        outgoing.reshape(row_count, CAP, SEGS * NT + 128), "row", split_axis=0, concat_axis=0, tiled=True
    ).reshape(row_count * CAP, SEGS * NT + 128)
    arrived_labels = arrived[:, SEGS * NT].astype(jnp.float32)
    wanted = jnp.arange(CH_DEV, dtype=jnp.float32)
    picking = (arrived_labels[None, :] == wanted[:, None]).astype(jnp.bfloat16)
    traces = jnp.dot(
        picking, arrived[:, : SEGS * NT], preferred_element_type=jnp.float32
    ).astype(jnp.bfloat16)
    row_own, col_own = spectra_of(traces.reshape(CH_DEV * SEGS, NT))
    col_spectra = lax.all_gather(col_own, "row", axis=0, tiled=True)
    row_spectra = lax.all_gather(row_own, "col", axis=0, tiled=True)
    row_total = row_spectra.shape[0]
    col_total = col_spectra.shape[0]
    col_local = jnp.arange(col_total, dtype=jnp.int32)
    col_ids = (col_local // CH_DEV * col_count + my_col) * CH_DEV + col_local % CH_DEV
    row_ids = my_row * col_count * CH_DEV + jnp.arange(row_total, dtype=jnp.int32)
    norm_scale = 1.0 / math.sqrt(SEGS * NF)
    keep = jnp.where(row_ids[:, None] != col_ids[None, :], norm_scale, 0.0).astype(jnp.float32)
    lagged = correlate(
        row_spectra, jnp.transpose(col_spectra, (1, 0, 2)), keep.reshape(-1, 1), lag_tables()
    )
    return lagged.reshape(row_total, col_total, LAGS)


def solution(mesh):
    placed = (P(("row", "col"), None), P(("row", "col")), P(("row", "col")), P(("row", "col")))
    return jax.shard_map(
        local, mesh=mesh, in_specs=placed, out_specs=P("row", "col", None), check_vma=False
    )
```

```python
import functools
import math

import jax
import jax.numpy as jnp
import numpy as np
from jax import lax
from jax.experimental import pallas as pl
from jax.experimental.pallas import tpu as pltpu
from jax.sharding import PartitionSpec as P

NF = 2048
NT = 4096
LAGS = 1024
SEGS = 8
CH_DEV = 4
CAP = 2
SMOOTH = 32
EDGE = 128
N1 = 16
N2 = NT // N1
F2 = NF // N1
HALF = LAGS // 2
PAIR = 2 * F2
STEPS = NF // PAIR
TILE = 256
TILES = 2 * HALF // TILE
MESH = pl.DeviceIdType.MESH


def forward_tables():
    n2 = np.arange(N2)
    f1 = np.arange(N1)
    f2 = np.arange(F2)
    angle = 2 * np.pi * (np.outer(f1, n2) % NT) / NT
    twiddle = np.stack([np.cos(angle), -np.sin(angle)]).astype(np.float32)
    angle = 2 * np.pi * (np.outer(n2, f2) % N2) / N2
    c, s = np.cos(angle), np.sin(angle)
    second = np.block([[c, -s], [s, c]]).astype(np.float32)
    high = second.astype(jnp.bfloat16)
    low = (second - high.astype(np.float32)).astype(jnp.bfloat16)
    f = f1[:, None] + N1 * f2[None, :]
    distance = np.minimum(f + 0.5, NF - f - 0.5)
    taper = np.sin(0.5 * np.pi * np.minimum(distance / EDGE, 1.0)) ** 2
    turn = np.pi * f / NT
    shape = np.stack([taper, np.cos(turn), -np.sin(turn)]).astype(np.float32)
    return twiddle, high, low, shape


def lag_tables():
    m2 = 2 * np.arange(HALF) + 1
    f1 = np.arange(N1)
    f2 = N1 * np.arange(F2)
    a = np.pi * (np.outer(f1, m2) % (2 * NT)) / NT
    b = np.pi * (np.outer(f2, m2) % (2 * NT)) / NT
    ac, as_, bc, bs = [jnp.asarray(t, jnp.float32) for t in (np.cos(a), np.sin(a), np.cos(b), np.sin(b))]
    c = ac[:, None] * bc[None] - as_[:, None] * bs[None]
    s = -(as_[:, None] * bc[None] + ac[:, None] * bs[None])
    c = c.reshape(STEPS, PAIR, HALF).astype(jnp.bfloat16)
    s = s.reshape(STEPS, PAIR, HALF).astype(jnp.bfloat16)
    parts = [t[:, :, k : k + TILE] for t in (c, s) for k in range(0, HALF, TILE)]
    return jnp.stack(parts, axis=1)


def shifted(value, lanes, amount):
    rolled = pltpu.roll(value, amount % F2, 1)
    source = lanes - amount
    return jnp.where((source >= 0) & (source < F2), rolled, 0.0)


def greet(axes):
    barrier = pltpu.get_barrier_semaphore()
    count = 0
    for axis in axes:
        size, me = lax.axis_size(axis), lax.axis_index(axis)
        for d in range(1, size):
            pl.semaphore_signal(barrier, inc=1, device_id={axis: lax.rem(me + d, size)}, device_id_type=MESH)
            count += 1
    pl.semaphore_wait(barrier, count)


def spectra_kernel(
    out_ref, tw_ref, hi_ref, lo_ref, shape_ref, row_ref, col_ref, got, x_ref, z_ref, send_sem, recv_sem
):
    size, me = lax.axis_size("row"), lax.axis_index("row")
    greet(("row",))

    def copy_of(d):
        peer = lax.rem(me + d, size)
        return pltpu.make_async_remote_copy(
            src_ref=out_ref.at[peer],
            dst_ref=got.at[d],
            send_sem=send_sem.at[d],
            recv_sem=recv_sem.at[d],
            device_id={"row": peer},
            device_id_type=MESH,
        )

    copies = [copy_of(d) for d in range(1, size)]
    for copy in copies:
        copy.start()
    got[0] = out_ref[me]
    for copy in copies:
        copy.wait()
    rows = x_ref.shape[0]
    slots = [(d, k) for d in range(size) for k in range(CAP)]
    label = [got[d, k, :, NT:].astype(jnp.float32) for d, k in slots]
    for ch in range(rows // SEGS):
        chosen = [v == np.float32(ch) for v in label]
        for h in range(0, NT, 128):
            total = None
            for (d, k), mask in zip(slots, chosen):
                term = jnp.where(mask, got[d, k, :, h : h + 128].astype(jnp.float32), 0.0)
                total = term if total is None else total + term
            x_ref[ch * SEGS : (ch + 1) * SEGS, h : h + 128] = total
    cosines = np.cos(2 * np.pi * np.arange(N1) / N1)
    sines = np.sin(2 * np.pi * np.arange(N1) / N1)

    def combine(values, weights):
        total = None
        for v, w in zip(values, weights):
            if abs(w) < 1e-9:
                continue
            term = v if abs(w - 1) < 1e-9 else (-v if abs(w + 1) < 1e-9 else v * np.float32(w))
            total = term if total is None else total + term
        return total

    for h in range(0, N2, 128):
        xs = [x_ref[:, k * N2 + h : k * N2 + h + 128] for k in range(N1)]
        even = [xs[k] + xs[k + N1 // 2] for k in range(N1 // 2)]
        odd = [xs[k] - xs[k + N1 // 2] for k in range(N1 // 2)]
        for f in range(N1 // 2 + 1):
            src = even if f % 2 == 0 else odd
            re = combine(src, [cosines[f * k % N1] for k in range(N1 // 2)])
            im = combine(src, [-sines[f * k % N1] for k in range(N1 // 2)])
            for f1, sign in {f: 1.0, (N1 - f) % N1: -1.0}.items() if f not in (0, N1 // 2) else ((f, 1.0),):
                tc = tw_ref[0, f1 : f1 + 1, h : h + 128]
                ts = tw_ref[1, f1 : f1 + 1, h : h + 128]
                if im is None:
                    zr, zi = re * tc, re * ts
                else:
                    i = im if sign > 0 else -im
                    zr, zi = re * tc - i * ts, re * ts + i * tc
                z_ref[f1 * rows : (f1 + 1) * rows, h : h + 128] = zr
                z_ref[f1 * rows : (f1 + 1) * rows, N2 + h : N2 + h + 128] = zi
    z = z_ref[...]
    zh = z.astype(jnp.bfloat16)
    zl = (z - zh.astype(jnp.float32)).astype(jnp.bfloat16)
    dot = functools.partial(jnp.dot, preferred_element_type=jnp.float32)
    z_ref[:, : 2 * F2] = dot(zh, hi_ref[...]) + dot(zl, hi_ref[...]) + dot(zh, lo_ref[...])

    lanes = lax.broadcasted_iota(jnp.int32, (rows, F2), 1)
    part = lambda f1, c: z_ref[f1 * rows : (f1 + 1) * rows, c * F2 : (c + 1) * F2]
    power = []
    for f1 in range(N1):
        re, im = part(f1, 0), part(f1, 1)
        power.append(re * re + im * im)
    prefix, suffix = [power[0]], [power[-1]]
    for k in range(1, N1):
        prefix.append(prefix[-1] + power[k])
        suffix.append(suffix[-1] + power[N1 - 1 - k])
    suffix = suffix[::-1]
    total = prefix[-1]
    reach = SMOOTH // N1
    middle = total
    for k in range(1, reach):
        middle = middle + shifted(total, lanes, k) + shifted(total, lanes, -k)
    for f1 in range(N1):
        window = middle + shifted(suffix[f1], lanes, reach) + shifted(prefix[f1], lanes, -reach)
        scale = shape_ref[0, f1 : f1 + 1] * lax.rsqrt(window * (1.0 / (2 * SMOOTH + 1)) + 1e-06)
        re, im = part(f1, 0) * scale, part(f1, 1) * scale
        tc, ts = shape_ref[1, f1 : f1 + 1], shape_ref[2, f1 : f1 + 1]
        tr, ti = re * tc - im * ts, re * ts + im * tc
        for ch in range(rows // SEGS):
            own = slice(ch * SEGS, (ch + 1) * SEGS)
            t, at = f1 * F2 // PAIR, slice(f1 * F2 % PAIR, f1 * F2 % PAIR + F2)
            col_ref[t, ch, :, at] = jnp.concatenate([re[own], im[own]], axis=0).astype(jnp.bfloat16)
            row_ref[t, ch, :, at] = jnp.concatenate([tr[own], ti[own]], axis=0).astype(jnp.bfloat16)


def spectra_of(outgoing):
    size = outgoing.shape[0]
    rows = CH_DEV * SEGS
    shape = jax.ShapeDtypeStruct((STEPS, CH_DEV, 2 * SEGS, PAIR), jnp.bfloat16)
    return pl.pallas_call(
        spectra_kernel,
        out_shape=(shape, shape),
        in_specs=[pl.BlockSpec(memory_space=pltpu.VMEM)] * 5,
        out_specs=[pl.BlockSpec(memory_space=pltpu.VMEM)] * 2,
        scratch_shapes=[
            pltpu.VMEM(outgoing.shape, jnp.bfloat16),
            pltpu.VMEM((rows, NT), jnp.float32),
            pltpu.VMEM((N1 * rows, 2 * N2), jnp.float32),
            pltpu.SemaphoreType.DMA((size,)),
            pltpu.SemaphoreType.DMA((size,)),
        ],
        compiler_params=pltpu.CompilerParams(
            vmem_limit_bytes=48 << 20, collective_id=0, has_side_effects=True
        ),
    )(outgoing, *[jnp.asarray(t) for t in forward_tables()])


def tree(terms):
    while len(terms) > 1:
        terms = [terms[k] + terms[k + 1] for k in range(0, len(terms), 2)]
    return terms[0]


def correlate_kernel(
    row_ref, col_ref, w_ref, keep_ref, flip_ref, out_ref, row_all, col_all, a32, b32, b_ref, cross, acc, sems
):
    row_total = row_all.shape[1] * CH_DEV
    col_total = col_all.shape[1] * CH_DEV
    share = row_total // TILES
    greet(("row", "col"))
    plans = []
    base = 0
    for axis, own, gathered in (("row", col_ref, col_all), ("col", row_ref, row_all)):
        size, me = lax.axis_size(axis), lax.axis_index(axis)
        for d in range(1, size):
            plans.append((axis, own, gathered, lax.rem(me + d, size), lax.rem(me + size - d, size), me, base + d - 1))
        base += size - 1

    def copy_of(plan, t, arriving):
        axis, own, gathered, peer, source, me, k = plan
        return pltpu.make_async_remote_copy(
            src_ref=own.at[t],
            dst_ref=gathered.at[t, source if arriving else me],
            send_sem=sems.at[0, k, t],
            recv_sem=sems.at[1, k, t],
            device_id={axis: peer},
            device_id_type=MESH,
        )

    @pl.loop(0, STEPS)
    def _(t):
        for plan in plans:
            copy_of(plan, t, False).start()

    row_me, col_me = lax.axis_index("row"), lax.axis_index("col")

    @pl.loop(0, STEPS)
    def _(t):
        col_all[t, row_me] = col_ref[t]
        row_all[t, col_me] = row_ref[t]

    def arrive(t):
        for plan in plans:
            copy_of(plan, t, True).wait_recv()
        a32[...] = row_all[t].reshape(a32.shape).astype(jnp.float32)
        for h in range(PAIR // F2):
            b32[h] = col_all[t, :, :, :, h * F2 : (h + 1) * F2].reshape(b32.shape[1:]).astype(jnp.float32)
            for k in range(2 * SEGS):
                rows = b32[h, pl.ds(k, col_total, stride=2 * SEGS), :]
                b_ref[k, :, h * F2 : (h + 1) * F2] = rows.astype(jnp.bfloat16)

    def cross_rows(first, now):
        for k in range(share):
            g = first + k
            for h in range(0, PAIR, F2):
                lane = slice(h, h + F2)
                real, imag = [], []
                for s in range(SEGS):
                    ar = jnp.broadcast_to(a32[g, s : s + 1, lane], (col_total, F2)).astype(jnp.bfloat16)
                    ai = jnp.broadcast_to(a32[g, SEGS + s : SEGS + s + 1, lane], (col_total, F2)).astype(jnp.bfloat16)
                    br, bi = b_ref[s, :, lane], b_ref[SEGS + s, :, lane]
                    real.append(ar * br + ai * bi)
                    imag.append(ai * br - ar * bi)
                at = pl.ds(pl.multiple_of(g * col_total, 16), col_total)
                cross[now, 0, at, lane] = tree(real)
                cross[now, 1, at, lane] = tree(imag)

    def lag_tile(i, t):
        before = lax.rem(t + 1, 2)
        part = jnp.dot(cross[before, i // (TILES // 2)], w_ref[t - 1, i], preferred_element_type=jnp.float32)
        acc[i] = acc[i] + part

    acc[...] = jnp.zeros_like(acc)
    arrive(0)

    @pl.loop(0, TILES)
    def _(i):
        cross_rows(i * share, 0)

    @pl.loop(1, STEPS)
    def _(t):
        arrive(t)

        @pl.loop(0, TILES)
        def _(i):
            lag_tile(i, t)
            cross_rows(i * share, lax.rem(t, 2))

    @pl.loop(0, TILES)
    def _(i):
        lag_tile(i, STEPS)

    keep = keep_ref[...]
    half = TILES // 2
    for k in range(half):
        up = (acc[k] + acc[half + k]) * keep
        down = (acc[k] - acc[half + k]) * keep
        out_ref[:, HALF + k * TILE : HALF + (k + 1) * TILE] = up.astype(jnp.bfloat16)
        turned = jnp.dot(down.astype(jnp.bfloat16), flip_ref[...], preferred_element_type=jnp.float32)
        out_ref[:, HALF - (k + 1) * TILE : HALF - k * TILE] = turned.astype(jnp.bfloat16)

    @pl.loop(0, STEPS)
    def _(t):
        for plan in plans:
            copy_of(plan, t, False).wait_send()


def correlate(row_own, col_own, keep, tables):
    row_count, col_count = lax.axis_size("row"), lax.axis_size("col")
    row_total, col_total = col_count * CH_DEV, row_count * CH_DEV
    pairs = row_total * col_total
    flip = np.eye(TILE, dtype=np.float32)[::-1]
    own = row_own.shape[1:]
    return pl.pallas_call(
        correlate_kernel,
        in_specs=[pl.BlockSpec(memory_space=pltpu.VMEM)] * 5,
        out_specs=pl.BlockSpec(memory_space=pltpu.VMEM),
        out_shape=jax.ShapeDtypeStruct((pairs, LAGS), jnp.bfloat16),
        scratch_shapes=[
            pltpu.VMEM((STEPS, col_count) + own, jnp.bfloat16),
            pltpu.VMEM((STEPS, row_count) + own, jnp.bfloat16),
            pltpu.VMEM((row_total, 2 * SEGS, PAIR), jnp.float32),
            pltpu.VMEM((PAIR // F2, col_total * 2 * SEGS, F2), jnp.float32),
            pltpu.VMEM((2 * SEGS, col_total, PAIR), jnp.bfloat16),
            pltpu.VMEM((2, 2, pairs, PAIR), jnp.bfloat16),
            pltpu.VMEM((TILES, pairs, TILE), jnp.float32),
            pltpu.SemaphoreType.DMA((2, row_count + col_count - 2, STEPS)),
        ],
        compiler_params=pltpu.CompilerParams(
            vmem_limit_bytes=58 << 20, collective_id=1, has_side_effects=True
        ),
    )(row_own, col_own, tables, keep, jnp.asarray(flip, jnp.bfloat16))


def local(strain, file_channels, file_counts, window_start):
    row_count = lax.axis_size("row")
    col_count = lax.axis_size("col")
    my_row = lax.axis_index("row")
    my_col = lax.axis_index("col")
    slot_total = strain.shape[0]
    window = lax.dynamic_slice_in_dim(strain, window_start[0], SEGS * NT, 1)
    slot_index = jnp.arange(slot_total, dtype=jnp.int32)
    live_slot = slot_index < file_counts[0]
    owner_row = file_channels // CH_DEV // col_count
    local_slot = file_channels % CH_DEV
    same_owner = (owner_row[:, None] == owner_row[None, :]) & live_slot[None, :]
    earlier = slot_index[None, :] < slot_index[:, None]
    position = jnp.sum((same_owner & earlier).astype(jnp.int32), axis=1)
    target = owner_row * CAP + position
    routing = (
        jnp.arange(row_count * CAP, dtype=jnp.int32)[:, None] == target[None, :]
    ) & live_slot[None, :]
    outgoing = jnp.dot(
        routing.astype(jnp.bfloat16), window, preferred_element_type=jnp.float32
    ).astype(jnp.bfloat16)
    labels = jnp.sum(jnp.where(routing, local_slot[None, :] + 1, 0), axis=1) - 1
    tail = jnp.broadcast_to(
        labels.astype(jnp.bfloat16)[:, None, None], (row_count * CAP, SEGS, 128)
    )
    outgoing = jnp.concatenate([outgoing.reshape(row_count * CAP, SEGS, NT), tail], axis=2)
    row_own, col_own = spectra_of(outgoing.reshape(row_count, CAP, SEGS, NT + 128))
    row_total = CH_DEV * col_count
    col_total = CH_DEV * row_count
    col_local = jnp.arange(col_total, dtype=jnp.int32)
    col_ids = (col_local // CH_DEV * col_count + my_col) * CH_DEV + col_local % CH_DEV
    row_ids = my_row * col_count * CH_DEV + jnp.arange(row_total, dtype=jnp.int32)
    norm_scale = 1.0 / math.sqrt(SEGS * NF)
    keep = jnp.where(row_ids[:, None] != col_ids[None, :], norm_scale, 0.0).astype(jnp.float32)
    lagged = correlate(row_own, col_own, keep.reshape(-1, 1), lag_tables())
    return lagged.reshape(row_total, col_total, LAGS)


def solution(mesh):
    placed = (P(("row", "col"), None), P(("row", "col")), P(("row", "col")), P(("row", "col")))
    return jax.shard_map(
        local, mesh=mesh, in_specs=placed, out_specs=P("row", "col", None), check_vma=False
    )
```

```python
import functools
import math

import jax
import jax.numpy as jnp
import numpy as np
from jax import lax
from jax.experimental import pallas as pl
from jax.experimental.pallas import tpu as pltpu
from jax.sharding import PartitionSpec as P

NF = 2048
NT = 4096
LAGS = 1024
SEGS = 8
CH_DEV = 4
CAP = 2
SMOOTH = 32
EDGE = 128
N1 = 16
N2 = NT // N1
F2 = NF // N1
HALF = LAGS // 2
PAIR = 2 * F2
STEPS = NF // PAIR
TILE = 256
TILES = 2 * HALF // TILE
MESH = pl.DeviceIdType.MESH


def forward_tables():
    n2 = np.arange(N2)
    f1 = np.arange(N1)
    f2 = np.arange(F2)
    angle = 2 * np.pi * (np.outer(f1, n2) % NT) / NT
    twiddle = np.stack([np.cos(angle), -np.sin(angle)]).astype(np.float32)
    angle = 2 * np.pi * (np.outer(n2, f2) % N2) / N2
    c, s = np.cos(angle), np.sin(angle)
    second = np.block([[c, -s], [s, c]]).astype(np.float32)
    high = second.astype(jnp.bfloat16)
    low = (second - high.astype(np.float32)).astype(jnp.bfloat16)
    f = f1[:, None] + N1 * f2[None, :]
    distance = np.minimum(f + 0.5, NF - f - 0.5)
    taper = np.sin(0.5 * np.pi * np.minimum(distance / EDGE, 1.0)) ** 2
    turn = np.pi * f / NT
    shape = np.stack([taper, np.cos(turn), -np.sin(turn)]).astype(np.float32)
    return twiddle, high, low, shape


def lag_tables():
    m2 = 2 * np.arange(HALF) + 1
    f1 = np.arange(N1)
    f2 = N1 * np.arange(F2)
    a = np.pi * (np.outer(f1, m2) % (2 * NT)) / NT
    b = np.pi * (np.outer(f2, m2) % (2 * NT)) / NT
    first = np.stack([np.cos(a), np.sin(a)]).astype(np.float32)
    second = np.stack([np.cos(b), np.sin(b)]).astype(np.float32)
    return first, second


def shifted(value, lanes, amount):
    rolled = pltpu.roll(value, amount % F2, 1)
    source = lanes - amount
    return jnp.where((source >= 0) & (source < F2), rolled, 0.0)


def greet(axes):
    barrier = pltpu.get_barrier_semaphore()
    count = 0
    for axis in axes:
        size, me = lax.axis_size(axis), lax.axis_index(axis)
        for d in range(1, size):
            pl.semaphore_signal(barrier, inc=1, device_id={axis: lax.rem(me + d, size)}, device_id_type=MESH)
            count += 1
    pl.semaphore_wait(barrier, count)


def spectra_kernel(out_ref, *refs):
    sources, rest = refs[:6], refs[6:]
    row_ref, col_ref, w_ref = rest[:3]
    tw_ref, hi_ref, lo_ref, shape_ref, first_ref, second_ref = consts = rest[3:9]
    got, x_ref, z_ref, send_sem, recv_sem, const_sem = rest[9:]
    loads = [pltpu.make_async_copy(f, t, const_sem.at[k]) for k, (f, t) in enumerate(zip(sources, consts))]
    for load in loads[::-1]:
        load.start()
    size, me = lax.axis_size("row"), lax.axis_index("row")
    greet(("row",))

    def copy_of(d):
        peer = lax.rem(me + d, size)
        return pltpu.make_async_remote_copy(
            src_ref=out_ref.at[peer],
            dst_ref=got.at[d],
            send_sem=send_sem.at[d],
            recv_sem=recv_sem.at[d],
            device_id={"row": peer},
            device_id_type=MESH,
        )

    copies = [copy_of(d) for d in range(1, size)]
    for copy in copies:
        copy.start()
    got[0] = out_ref[me]
    for load in loads:
        load.wait()
    for k in range(HALF // TILE):
        lane = slice(k * TILE, (k + 1) * TILE)
        bc, bs = second_ref[0, :, lane], second_ref[1, :, lane]
        for f1 in range(N1):
            ac, as_ = first_ref[0, f1 : f1 + 1, lane], first_ref[1, f1 : f1 + 1, lane]
            t, at = f1 * F2 // PAIR, slice(f1 * F2 % PAIR, f1 * F2 % PAIR + F2)
            w_ref[t, k, at, :] = (ac * bc - as_ * bs).astype(jnp.bfloat16)
            w_ref[t, HALF // TILE + k, at, :] = (-(as_ * bc + ac * bs)).astype(jnp.bfloat16)
    for copy in copies:
        copy.wait()
    rows = x_ref.shape[0]
    slots = [(d, k) for d in range(size) for k in range(CAP)]
    label = [got[d, k, :, NT:].astype(jnp.float32) for d, k in slots]
    for ch in range(rows // SEGS):
        chosen = [v == np.float32(ch) for v in label]
        for h in range(0, NT, 128):
            total = None
            for (d, k), mask in zip(slots, chosen):
                term = jnp.where(mask, got[d, k, :, h : h + 128].astype(jnp.float32), 0.0)
                total = term if total is None else total + term
            x_ref[ch * SEGS : (ch + 1) * SEGS, h : h + 128] = total
    cosines = np.cos(2 * np.pi * np.arange(N1) / N1)
    sines = np.sin(2 * np.pi * np.arange(N1) / N1)

    def combine(values, weights):
        total = None
        for v, w in zip(values, weights):
            if abs(w) < 1e-9:
                continue
            term = v if abs(w - 1) < 1e-9 else (-v if abs(w + 1) < 1e-9 else v * np.float32(w))
            total = term if total is None else total + term
        return total

    for h in range(0, N2, 128):
        xs = [x_ref[:, k * N2 + h : k * N2 + h + 128] for k in range(N1)]
        even = [xs[k] + xs[k + N1 // 2] for k in range(N1 // 2)]
        odd = [xs[k] - xs[k + N1 // 2] for k in range(N1 // 2)]
        for f in range(N1 // 2 + 1):
            src = even if f % 2 == 0 else odd
            re = combine(src, [cosines[f * k % N1] for k in range(N1 // 2)])
            im = combine(src, [-sines[f * k % N1] for k in range(N1 // 2)])
            for f1, sign in {f: 1.0, (N1 - f) % N1: -1.0}.items() if f not in (0, N1 // 2) else ((f, 1.0),):
                tc = tw_ref[0, f1 : f1 + 1, h : h + 128]
                ts = tw_ref[1, f1 : f1 + 1, h : h + 128]
                if im is None:
                    zr, zi = re * tc, re * ts
                else:
                    i = im if sign > 0 else -im
                    zr, zi = re * tc - i * ts, re * ts + i * tc
                z_ref[f1 * rows : (f1 + 1) * rows, h : h + 128] = zr
                z_ref[f1 * rows : (f1 + 1) * rows, N2 + h : N2 + h + 128] = zi
    z = z_ref[...]
    zh = z.astype(jnp.bfloat16)
    zl = (z - zh.astype(jnp.float32)).astype(jnp.bfloat16)
    dot = functools.partial(jnp.dot, preferred_element_type=jnp.float32)
    z_ref[:, : 2 * F2] = dot(zh, hi_ref[...]) + dot(zl, hi_ref[...]) + dot(zh, lo_ref[...])

    lanes = lax.broadcasted_iota(jnp.int32, (rows, F2), 1)
    part = lambda f1, c: z_ref[f1 * rows : (f1 + 1) * rows, c * F2 : (c + 1) * F2]
    power = []
    for f1 in range(N1):
        re, im = part(f1, 0), part(f1, 1)
        power.append(re * re + im * im)
    prefix, suffix = [power[0]], [power[-1]]
    for k in range(1, N1):
        prefix.append(prefix[-1] + power[k])
        suffix.append(suffix[-1] + power[N1 - 1 - k])
    suffix = suffix[::-1]
    total = prefix[-1]
    reach = SMOOTH // N1
    middle = total
    for k in range(1, reach):
        middle = middle + shifted(total, lanes, k) + shifted(total, lanes, -k)
    for f1 in range(N1):
        window = middle + shifted(suffix[f1], lanes, reach) + shifted(prefix[f1], lanes, -reach)
        scale = shape_ref[0, f1 : f1 + 1] * lax.rsqrt(window * (1.0 / (2 * SMOOTH + 1)) + 1e-06)
        re, im = part(f1, 0) * scale, part(f1, 1) * scale
        tc, ts = shape_ref[1, f1 : f1 + 1], shape_ref[2, f1 : f1 + 1]
        tr, ti = re * tc - im * ts, re * ts + im * tc
        for ch in range(rows // SEGS):
            own = slice(ch * SEGS, (ch + 1) * SEGS)
            t, at = f1 * F2 // PAIR, slice(f1 * F2 % PAIR, f1 * F2 % PAIR + F2)
            col_ref[t, ch, :, at] = jnp.concatenate([re[own], im[own]], axis=0).astype(jnp.bfloat16)
            row_ref[t, ch, :, at] = jnp.concatenate([tr[own], ti[own]], axis=0).astype(jnp.bfloat16)


def spectra_of(outgoing):
    size = outgoing.shape[0]
    consts = [jnp.asarray(t) for t in forward_tables() + lag_tables()]
    rows = CH_DEV * SEGS
    shape = jax.ShapeDtypeStruct((STEPS, CH_DEV, 2 * SEGS, PAIR), jnp.bfloat16)
    return pl.pallas_call(
        spectra_kernel,
        out_shape=(shape, shape, jax.ShapeDtypeStruct((STEPS, TILES, PAIR, TILE), jnp.bfloat16)),
        in_specs=[pl.BlockSpec(memory_space=pltpu.VMEM)] + [pl.BlockSpec(memory_space=pl.ANY)] * len(consts),
        out_specs=[pl.BlockSpec(memory_space=pltpu.VMEM)] * 3,
        scratch_shapes=[pltpu.VMEM(t.shape, t.dtype) for t in consts]
        + [
            pltpu.VMEM(outgoing.shape, jnp.bfloat16),
            pltpu.VMEM((rows, NT), jnp.float32),
            pltpu.VMEM((N1 * rows, 2 * N2), jnp.float32),
            pltpu.SemaphoreType.DMA((size,)),
            pltpu.SemaphoreType.DMA((size,)),
            pltpu.SemaphoreType.DMA((len(consts),)),
        ],
        compiler_params=pltpu.CompilerParams(
            vmem_limit_bytes=48 << 20, collective_id=0, has_side_effects=True
        ),
    )(outgoing, *consts)


def tree(terms):
    while len(terms) > 1:
        terms = [terms[k] + terms[k + 1] for k in range(0, len(terms), 2)]
    return terms[0]


def correlate_kernel(
    row_ref, col_ref, w_ref, flip_ref, out_hbm, row_all, col_all, a32, b32, b_ref, cross, acc, out_ref, sems, out_sem
):
    row_total = row_all.shape[1] * CH_DEV
    col_total = col_all.shape[1] * CH_DEV
    share = row_total // TILES
    greet(("row", "col"))
    plans = []
    base = 0
    for axis, own, gathered in (("row", col_ref, col_all), ("col", row_ref, row_all)):
        size, me = lax.axis_size(axis), lax.axis_index(axis)
        for d in range(1, size):
            plans.append((axis, own, gathered, lax.rem(me + d, size), lax.rem(me + size - d, size), me, base + d - 1))
        base += size - 1

    def copy_of(plan, t, arriving):
        axis, own, gathered, peer, source, me, k = plan
        return pltpu.make_async_remote_copy(
            src_ref=own.at[t],
            dst_ref=gathered.at[t, source if arriving else me],
            send_sem=sems.at[0, k, t],
            recv_sem=sems.at[1, k, t],
            device_id={axis: peer},
            device_id_type=MESH,
        )

    @pl.loop(0, STEPS)
    def _(t):
        for plan in plans:
            copy_of(plan, t, False).start()

    row_me, col_me = lax.axis_index("row"), lax.axis_index("col")

    @pl.loop(0, STEPS)
    def _(t):
        col_all[t, row_me] = col_ref[t]
        row_all[t, col_me] = row_ref[t]

    def arrive(t):
        for plan in plans:
            copy_of(plan, t, True).wait_recv()
        a32[...] = row_all[t].reshape(a32.shape).astype(jnp.float32)
        for h in range(PAIR // F2):
            b32[h] = col_all[t, :, :, :, h * F2 : (h + 1) * F2].reshape(b32.shape[1:]).astype(jnp.float32)
            for k in range(2 * SEGS):
                rows = b32[h, pl.ds(k, col_total, stride=2 * SEGS), :]
                b_ref[k, :, h * F2 : (h + 1) * F2] = rows.astype(jnp.bfloat16)

    def cross_rows(first, now):
        for k in range(share):
            g = first + k
            for h in range(0, PAIR, F2):
                lane = slice(h, h + F2)
                real, imag = [], []
                for s in range(SEGS):
                    ar = jnp.broadcast_to(a32[g, s : s + 1, lane], (col_total, F2)).astype(jnp.bfloat16)
                    ai = jnp.broadcast_to(a32[g, SEGS + s : SEGS + s + 1, lane], (col_total, F2)).astype(jnp.bfloat16)
                    br, bi = b_ref[s, :, lane], b_ref[SEGS + s, :, lane]
                    real.append(ar * br + ai * bi)
                    imag.append(ai * br - ar * bi)
                at = pl.ds(pl.multiple_of(g * col_total, 16), col_total)
                cross[now, 0, at, lane] = tree(real)
                cross[now, 1, at, lane] = tree(imag)

    def lag_tile(i, t):
        before = lax.rem(t + 1, 2)
        part = jnp.dot(cross[before, i // (TILES // 2)], w_ref[t - 1, i], preferred_element_type=jnp.float32)
        acc[i] = acc[i] + part

    acc[...] = jnp.zeros_like(acc)
    arrive(0)

    @pl.loop(0, TILES)
    def _(i):
        cross_rows(i * share, 0)

    @pl.loop(1, STEPS)
    def _(t):
        arrive(t)

        @pl.loop(0, TILES)
        def _(i):
            lag_tile(i, t)
            cross_rows(i * share, lax.rem(t, 2))

    @pl.loop(0, TILES)
    def _(i):
        lag_tile(i, STEPS)

    pairs = row_total * col_total
    place = lax.broadcasted_iota(jnp.int32, (pairs, TILE), 0) - (col_me * col_total + row_me) * CH_DEV
    same = place == 0
    for ch in range(1, CH_DEV):
        same = same | (place == ch * (col_total + 1))
    keep = jnp.where(same, 0.0, np.float32(1.0 / math.sqrt(SEGS * NF)))
    half = TILES // 2
    leaving = []

    def leave(first):
        lane = pl.ds(first, TILE)
        copy = pltpu.make_async_copy(out_ref.at[:, lane], out_hbm.at[:, lane], out_sem.at[first // TILE])
        copy.start()
        leaving.append(copy)

    for k in range(half):
        up = (acc[k] + acc[half + k]) * keep
        down = (acc[k] - acc[half + k]) * keep
        out_ref[:, HALF + k * TILE : HALF + (k + 1) * TILE] = up.astype(jnp.bfloat16)
        leave(HALF + k * TILE)
        turned = jnp.dot(down.astype(jnp.bfloat16), flip_ref[...], preferred_element_type=jnp.float32)
        out_ref[:, HALF - (k + 1) * TILE : HALF - k * TILE] = turned.astype(jnp.bfloat16)
        leave(HALF - (k + 1) * TILE)
    for copy in leaving:
        copy.wait()

    @pl.loop(0, STEPS)
    def _(t):
        for plan in plans:
            copy_of(plan, t, False).wait_send()


def correlate(row_own, col_own, tables):
    row_count, col_count = lax.axis_size("row"), lax.axis_size("col")
    row_total, col_total = col_count * CH_DEV, row_count * CH_DEV
    pairs = row_total * col_total
    flip = np.eye(TILE, dtype=np.float32)[::-1]
    own = row_own.shape[1:]
    return pl.pallas_call(
        correlate_kernel,
        in_specs=[pl.BlockSpec(memory_space=pltpu.VMEM)] * 4,
        out_specs=pl.BlockSpec(memory_space=pl.ANY),
        out_shape=jax.ShapeDtypeStruct((pairs, LAGS), jnp.bfloat16),
        scratch_shapes=[
            pltpu.VMEM((STEPS, col_count) + own, jnp.bfloat16),
            pltpu.VMEM((STEPS, row_count) + own, jnp.bfloat16),
            pltpu.VMEM((row_total, 2 * SEGS, PAIR), jnp.float32),
            pltpu.VMEM((PAIR // F2, col_total * 2 * SEGS, F2), jnp.float32),
            pltpu.VMEM((2 * SEGS, col_total, PAIR), jnp.bfloat16),
            pltpu.VMEM((2, 2, pairs, PAIR), jnp.bfloat16),
            pltpu.VMEM((TILES, pairs, TILE), jnp.float32),
            pltpu.VMEM((pairs, LAGS), jnp.bfloat16),
            pltpu.SemaphoreType.DMA((2, row_count + col_count - 2, STEPS)),
            pltpu.SemaphoreType.DMA((LAGS // TILE,)),
        ],
        compiler_params=pltpu.CompilerParams(
            vmem_limit_bytes=58 << 20, collective_id=1, has_side_effects=True
        ),
    )(row_own, col_own, tables, jnp.asarray(flip, jnp.bfloat16))


def local(strain, file_channels, file_counts, window_start):
    row_count = lax.axis_size("row")
    col_count = lax.axis_size("col")
    my_row = lax.axis_index("row")
    my_col = lax.axis_index("col")
    slot_total = strain.shape[0]
    window = lax.dynamic_slice_in_dim(strain, window_start[0], SEGS * NT, 1)
    slot_index = jnp.arange(slot_total, dtype=jnp.int32)
    live_slot = slot_index < file_counts[0]
    owner_row = file_channels // CH_DEV // col_count
    local_slot = file_channels % CH_DEV
    same_owner = (owner_row[:, None] == owner_row[None, :]) & live_slot[None, :]
    earlier = slot_index[None, :] < slot_index[:, None]
    position = jnp.sum((same_owner & earlier).astype(jnp.int32), axis=1)
    target = owner_row * CAP + position
    routing = (
        jnp.arange(row_count * CAP, dtype=jnp.int32)[:, None] == target[None, :]
    ) & live_slot[None, :]
    outgoing = jnp.dot(
        routing.astype(jnp.bfloat16), window, preferred_element_type=jnp.float32
    ).astype(jnp.bfloat16)
    labels = jnp.sum(jnp.where(routing, local_slot[None, :] + 1, 0), axis=1) - 1
    tail = jnp.broadcast_to(
        labels.astype(jnp.bfloat16)[:, None, None], (row_count * CAP, SEGS, 128)
    )
    outgoing = jnp.concatenate([outgoing.reshape(row_count * CAP, SEGS, NT), tail], axis=2)
    row_own, col_own, tables = spectra_of(outgoing.reshape(row_count, CAP, SEGS, NT + 128))
    row_total = CH_DEV * col_count
    col_total = CH_DEV * row_count
    lagged = correlate(row_own, col_own, tables)
    return lagged.reshape(row_total, col_total, LAGS)


def solution(mesh):
    placed = (P(("row", "col"), None), P(("row", "col")), P(("row", "col")), P(("row", "col")))
    return jax.shard_map(
        local, mesh=mesh, in_specs=placed, out_specs=P("row", "col", None), check_vma=False
    )
```

```python
import functools
import math

import jax
import jax.numpy as jnp
import numpy as np
from jax import lax
from jax.experimental import pallas as pl
from jax.experimental.pallas import tpu as pltpu
from jax.sharding import PartitionSpec as P

NF = 2048
NT = 4096
LAGS = 1024
SEGS = 8
CH_DEV = 4
CAP = 2
SMOOTH = 32
EDGE = 128
N1 = 16
N2 = NT // N1
F2 = NF // N1
HALF = LAGS // 2
PAIR = 2 * F2
STEPS = NF // PAIR
TILE = 256
TILES = 2 * HALF // TILE
AHEAD = 2
MESH = pl.DeviceIdType.MESH


def forward_tables():
    n2 = np.arange(N2)
    f1 = np.arange(N1)
    f2 = np.arange(F2)
    angle = 2 * np.pi * (np.outer(f1, n2) % NT) / NT
    twiddle = np.stack([np.cos(angle), -np.sin(angle)]).astype(np.float32)
    angle = 2 * np.pi * (np.outer(n2, f2) % N2) / N2
    c, s = np.cos(angle), np.sin(angle)
    second = np.block([[c, -s], [s, c]]).astype(np.float32)
    high = second.astype(jnp.bfloat16)
    low = (second - high.astype(np.float32)).astype(jnp.bfloat16)
    f = f1[:, None] + N1 * f2[None, :]
    distance = np.minimum(f + 0.5, NF - f - 0.5)
    taper = np.sin(0.5 * np.pi * np.minimum(distance / EDGE, 1.0)) ** 2
    turn = np.pi * f / NT
    shape = np.stack([taper, np.cos(turn), -np.sin(turn)]).astype(np.float32)
    return twiddle, high, low, shape


def lag_tables():
    m2 = 2 * np.arange(HALF) + 1
    f1 = np.arange(N1)
    f2 = N1 * np.arange(F2)
    a = np.pi * (np.outer(f1, m2) % (2 * NT)) / NT
    b = np.pi * (np.outer(f2, m2) % (2 * NT)) / NT
    first = np.stack([np.cos(a), np.sin(a)]).astype(np.float32)
    second = np.stack([np.cos(b), np.sin(b)]).astype(np.float32)
    return first, second


def shifted(value, lanes, amount):
    rolled = pltpu.roll(value, amount % F2, 1)
    source = lanes - amount
    return jnp.where((source >= 0) & (source < F2), rolled, 0.0)


def greet(axes):
    barrier = pltpu.get_barrier_semaphore()
    count = 0
    for axis in axes:
        size, me = lax.axis_size(axis), lax.axis_index(axis)
        for d in range(1, size):
            pl.semaphore_signal(barrier, inc=1, device_id={axis: lax.rem(me + d, size)}, device_id_type=MESH)
            count += 1
    pl.semaphore_wait(barrier, count)


def spectra_kernel(out_ref, *refs):
    sources, rest = refs[:6], refs[6:]
    row_ref, col_ref, w_ref = rest[:3]
    tw_ref, hi_ref, lo_ref, shape_ref, first_ref, second_ref = consts = rest[3:9]
    got, x_ref, z_ref, send_sem, recv_sem, const_sem = rest[9:]
    loads = [pltpu.make_async_copy(f, t, const_sem.at[k]) for k, (f, t) in enumerate(zip(sources, consts))]
    for load in loads[::-1]:
        load.start()
    size, me = lax.axis_size("row"), lax.axis_index("row")
    greet(("row",))

    def copy_of(d):
        peer = lax.rem(me + d, size)
        return pltpu.make_async_remote_copy(
            src_ref=out_ref.at[peer],
            dst_ref=got.at[d],
            send_sem=send_sem.at[d],
            recv_sem=recv_sem.at[d],
            device_id={"row": peer},
            device_id_type=MESH,
        )

    copies = [copy_of(d) for d in range(1, size)]
    for copy in copies:
        copy.start()
    got[0] = out_ref[me]
    for load in loads:
        load.wait()
    for k in range(HALF // TILE):
        lane = slice(k * TILE, (k + 1) * TILE)
        bc, bs = second_ref[0, :, lane], second_ref[1, :, lane]
        for f1 in range(N1):
            ac, as_ = first_ref[0, f1 : f1 + 1, lane], first_ref[1, f1 : f1 + 1, lane]
            t, at = f1 * F2 // PAIR, slice(f1 * F2 % PAIR, f1 * F2 % PAIR + F2)
            w_ref[t, k, at, :] = (ac * bc - as_ * bs).astype(jnp.bfloat16)
            w_ref[t, HALF // TILE + k, at, :] = (-(as_ * bc + ac * bs)).astype(jnp.bfloat16)
    for copy in copies:
        copy.wait()
    rows = x_ref.shape[0]
    slots = [(d, k) for d in range(size) for k in range(CAP)]
    label = [got[d, k, :, NT:].astype(jnp.float32) for d, k in slots]
    for ch in range(rows // SEGS):
        chosen = [v == np.float32(ch) for v in label]
        for h in range(0, NT, 128):
            total = None
            for (d, k), mask in zip(slots, chosen):
                term = jnp.where(mask, got[d, k, :, h : h + 128].astype(jnp.float32), 0.0)
                total = term if total is None else total + term
            x_ref[ch * SEGS : (ch + 1) * SEGS, h : h + 128] = total
    cosines = np.cos(2 * np.pi * np.arange(N1) / N1)
    sines = np.sin(2 * np.pi * np.arange(N1) / N1)

    def combine(values, weights):
        total = None
        for v, w in zip(values, weights):
            if abs(w) < 1e-9:
                continue
            term = v if abs(w - 1) < 1e-9 else (-v if abs(w + 1) < 1e-9 else v * np.float32(w))
            total = term if total is None else total + term
        return total

    for h in range(0, N2, 128):
        xs = [x_ref[:, k * N2 + h : k * N2 + h + 128] for k in range(N1)]
        even = [xs[k] + xs[k + N1 // 2] for k in range(N1 // 2)]
        odd = [xs[k] - xs[k + N1 // 2] for k in range(N1 // 2)]
        for f in range(N1 // 2 + 1):
            src = even if f % 2 == 0 else odd
            re = combine(src, [cosines[f * k % N1] for k in range(N1 // 2)])
            im = combine(src, [-sines[f * k % N1] for k in range(N1 // 2)])
            for f1, sign in {f: 1.0, (N1 - f) % N1: -1.0}.items() if f not in (0, N1 // 2) else ((f, 1.0),):
                tc = tw_ref[0, f1 : f1 + 1, h : h + 128]
                ts = tw_ref[1, f1 : f1 + 1, h : h + 128]
                if im is None:
                    zr, zi = re * tc, re * ts
                else:
                    i = im if sign > 0 else -im
                    zr, zi = re * tc - i * ts, re * ts + i * tc
                z_ref[f1 * rows : (f1 + 1) * rows, h : h + 128] = zr
                z_ref[f1 * rows : (f1 + 1) * rows, N2 + h : N2 + h + 128] = zi
    z = z_ref[...]
    zh = z.astype(jnp.bfloat16)
    zl = (z - zh.astype(jnp.float32)).astype(jnp.bfloat16)
    dot = functools.partial(jnp.dot, preferred_element_type=jnp.float32)
    z_ref[:, : 2 * F2] = dot(zh, hi_ref[...]) + dot(zl, hi_ref[...]) + dot(zh, lo_ref[...])

    lanes = lax.broadcasted_iota(jnp.int32, (rows, F2), 1)
    part = lambda f1, c: z_ref[f1 * rows : (f1 + 1) * rows, c * F2 : (c + 1) * F2]
    power = []
    for f1 in range(N1):
        re, im = part(f1, 0), part(f1, 1)
        power.append(re * re + im * im)
    prefix, suffix = [power[0]], [power[-1]]
    for k in range(1, N1):
        prefix.append(prefix[-1] + power[k])
        suffix.append(suffix[-1] + power[N1 - 1 - k])
    suffix = suffix[::-1]
    total = prefix[-1]
    reach = SMOOTH // N1
    middle = total
    for k in range(1, reach):
        middle = middle + shifted(total, lanes, k) + shifted(total, lanes, -k)
    for f1 in range(N1):
        window = middle + shifted(suffix[f1], lanes, reach) + shifted(prefix[f1], lanes, -reach)
        scale = shape_ref[0, f1 : f1 + 1] * lax.rsqrt(window * (1.0 / (2 * SMOOTH + 1)) + 1e-06)
        re, im = part(f1, 0) * scale, part(f1, 1) * scale
        tc, ts = shape_ref[1, f1 : f1 + 1], shape_ref[2, f1 : f1 + 1]
        tr, ti = re * tc - im * ts, re * ts + im * tc
        for ch in range(rows // SEGS):
            own = slice(ch * SEGS, (ch + 1) * SEGS)
            t, at = f1 * F2 // PAIR, slice(f1 * F2 % PAIR, f1 * F2 % PAIR + F2)
            col_ref[t, ch, :, at] = jnp.concatenate([re[own], im[own]], axis=0).astype(jnp.bfloat16)
            row_ref[t, ch, :, at] = jnp.concatenate([tr[own], ti[own]], axis=0).astype(jnp.bfloat16)


def spectra_of(outgoing):
    size = outgoing.shape[0]
    consts = [jnp.asarray(t) for t in forward_tables() + lag_tables()]
    rows = CH_DEV * SEGS
    shape = jax.ShapeDtypeStruct((STEPS, CH_DEV, 2 * SEGS, PAIR), jnp.bfloat16)
    return pl.pallas_call(
        spectra_kernel,
        out_shape=(shape, shape, jax.ShapeDtypeStruct((STEPS, TILES, PAIR, TILE), jnp.bfloat16)),
        in_specs=[pl.BlockSpec(memory_space=pltpu.VMEM)] + [pl.BlockSpec(memory_space=pl.ANY)] * len(consts),
        out_specs=[pl.BlockSpec(memory_space=pltpu.VMEM)] * 3,
        scratch_shapes=[pltpu.VMEM(t.shape, t.dtype) for t in consts]
        + [
            pltpu.VMEM(outgoing.shape, jnp.bfloat16),
            pltpu.VMEM((rows, NT), jnp.float32),
            pltpu.VMEM((N1 * rows, 2 * N2), jnp.float32),
            pltpu.SemaphoreType.DMA((size,)),
            pltpu.SemaphoreType.DMA((size,)),
            pltpu.SemaphoreType.DMA((len(consts),)),
        ],
        compiler_params=pltpu.CompilerParams(
            vmem_limit_bytes=48 << 20, collective_id=0, has_side_effects=True
        ),
    )(outgoing, *consts)


def tree(terms):
    while len(terms) > 1:
        terms = [terms[k] + terms[k + 1] for k in range(0, len(terms), 2)]
    return terms[0]


def correlate_kernel(
    row_ref, col_ref, w_ref, flip_ref, out_hbm, row_all, col_all, a32, b32, b_ref, cross, acc, out_ref, sems, out_sem
):
    row_total = row_all.shape[1] * CH_DEV
    col_total = col_all.shape[1] * CH_DEV
    share = row_total // TILES
    row_me, col_me = lax.axis_index("row"), lax.axis_index("col")
    row_size, col_size = lax.axis_size("row"), lax.axis_size("col")
    partner = col_me + 1 - 2 * lax.rem(col_me, 2)
    groups = col_size // 2
    lag = row_size - 2
    greet(("row", "col"))

    def always(act):
        act()

    hops = []
    for step in (1, -1):
        for d in range(row_size - 1):
            behind, last = row_me - step * d, row_me - step * (d + 1)
            inside = lambda r: (r >= 0) & (r < row_size)
            may_send = inside(behind) & inside(row_me + step)
            hops.append((pl.when(may_send), pl.when(inside(last)), "row", row_me + step, behind, last, d))
    for d in range(1, groups):
        peer, source = lax.rem(col_me + 2 * d, col_size), lax.rem(col_me + col_size - 2 * d, col_size)
        hops.append((always, always, "col", peer, col_me, source, 0))
    for d in range(groups):
        mine, other = [lax.rem(r + col_size - 2 * d, col_size) for r in (col_me, partner)]
        hops.append((always, always, "col", partner, mine, other, -1 if d else 0))

    def copy_of(k, t, arriving):
        _, _, axis, peer, slot, source, passed = hops[k]
        gathered, own = (col_all, col_ref) if axis == "row" else (row_all, row_ref)
        place = gathered.at[t, source if arriving else slot]
        return pltpu.make_async_remote_copy(
            src_ref=own.at[t] if passed == 0 and not arriving else place,
            dst_ref=place,
            send_sem=sems.at[0, k, t],
            recv_sem=sems.at[1, k, t],
            device_id={axis: peer},
            device_id_type=MESH,
        )

    def on_send(k, act):
        hops[k][0](act)

    def on_arrival(k, act):
        hops[k][1](act)

    own_hops = [k for k, hop in enumerate(hops) if hop[6] == 0]

    def send_own(t):
        for k in own_hops:
            on_send(k, lambda k=k: copy_of(k, t, False).start())

    def within(t):
        return always if isinstance(t, int) else pl.when(t < STEPS)

    def exchange(p):
        for d in range(row_size - 1):
            t = p - d
            if isinstance(t, int) and t < 0:
                continue

            def serve(d=d, t=t):
                for side in range(2):
                    k = side * (row_size - 1) + d
                    on_arrival(k, lambda k=k: copy_of(k, t, True).wait_recv())
                    if d + 1 < row_size - 1:
                        on_send(k + 1, lambda k=k: copy_of(k + 1, t, False).start())

            within(t)(serve)
        base = 2 * (row_size - 1)
        t = p - max(lag - 1, 0)
        if not isinstance(t, int) or t >= 0:

            def serve_col(t=t):
                for d in range(1, groups):
                    copy_of(base + d - 1, t, True).wait_recv()
                    copy_of(base + groups - 1 + d, t, False).start()

            within(t)(serve_col)
        t = p + AHEAD
        within(t)(lambda: send_own(t))

    for t in range(AHEAD):
        send_own(t)

    @pl.loop(0, STEPS)
    def _(t):
        col_all[t, row_me] = col_ref[t]
        row_all[t, col_me] = row_ref[t]

    for p in range(lag):
        exchange(p)

    def arrive(t):
        exchange(t + lag)
        for d in range(groups):
            copy_of(2 * (row_size - 1) + groups - 1 + d, t, True).wait_recv()
        a32[...] = row_all[t].reshape(a32.shape).astype(jnp.float32)
        for h in range(PAIR // F2):
            b32[h] = col_all[t, :, :, :, h * F2 : (h + 1) * F2].reshape(b32.shape[1:]).astype(jnp.float32)
            for k in range(2 * SEGS):
                rows = b32[h, pl.ds(k, col_total, stride=2 * SEGS), :]
                b_ref[k, :, h * F2 : (h + 1) * F2] = rows.astype(jnp.bfloat16)

    def cross_rows(first, now):
        for k in range(share):
            g = first + k
            for h in range(0, PAIR, F2):
                lane = slice(h, h + F2)
                real, imag = [], []
                for s in range(SEGS):
                    ar = jnp.broadcast_to(a32[g, s : s + 1, lane], (col_total, F2)).astype(jnp.bfloat16)
                    ai = jnp.broadcast_to(a32[g, SEGS + s : SEGS + s + 1, lane], (col_total, F2)).astype(jnp.bfloat16)
                    br, bi = b_ref[s, :, lane], b_ref[SEGS + s, :, lane]
                    real.append(ar * br + ai * bi)
                    imag.append(ai * br - ar * bi)
                at = pl.ds(pl.multiple_of(g * col_total, 16), col_total)
                cross[now, 0, at, lane] = tree(real)
                cross[now, 1, at, lane] = tree(imag)

    def lag_tile(i, t):
        before = lax.rem(t + 1, 2)
        part = jnp.dot(cross[before, i // (TILES // 2)], w_ref[t - 1, i], preferred_element_type=jnp.float32)
        acc[i] = acc[i] + part

    acc[...] = jnp.zeros_like(acc)
    arrive(0)

    @pl.loop(0, TILES)
    def _(i):
        cross_rows(i * share, 0)

    @pl.loop(1, STEPS)
    def _(t):
        arrive(t)

        @pl.loop(0, TILES)
        def _(i):
            lag_tile(i, t)
            cross_rows(i * share, lax.rem(t, 2))

    @pl.loop(0, TILES)
    def _(i):
        lag_tile(i, STEPS)

    pairs = row_total * col_total
    place = lax.broadcasted_iota(jnp.int32, (pairs, TILE), 0) - (col_me * col_total + row_me) * CH_DEV
    same = place == 0
    for ch in range(1, CH_DEV):
        same = same | (place == ch * (col_total + 1))
    keep = jnp.where(same, 0.0, np.float32(1.0 / math.sqrt(SEGS * NF)))
    half = TILES // 2
    leaving = []

    def leave(first):
        lane = pl.ds(first, TILE)
        copy = pltpu.make_async_copy(out_ref.at[:, :, lane], out_hbm.at[:, :, lane], out_sem.at[first // TILE])
        copy.start()
        leaving.append(copy)

    for k in range(half):
        up = (acc[k] + acc[half + k]) * keep
        down = (acc[k] - acc[half + k]) * keep
        out_ref[:, :, HALF + k * TILE : HALF + (k + 1) * TILE] = (
            up.reshape(row_total, col_total, TILE).astype(jnp.bfloat16)
        )
        leave(HALF + k * TILE)
        turned = jnp.dot(down.astype(jnp.bfloat16), flip_ref[...], preferred_element_type=jnp.float32)
        out_ref[:, :, HALF - (k + 1) * TILE : HALF - k * TILE] = (
            turned.reshape(row_total, col_total, TILE).astype(jnp.bfloat16)
        )
        leave(HALF - (k + 1) * TILE)
    for copy in leaving:
        copy.wait()

    @pl.loop(0, STEPS)
    def _(t):
        for k in range(len(hops)):
            on_send(k, lambda k=k: copy_of(k, t, False).wait_send())


def correlate(row_own, col_own, tables):
    row_count, col_count = lax.axis_size("row"), lax.axis_size("col")
    row_total, col_total = col_count * CH_DEV, row_count * CH_DEV
    pairs = row_total * col_total
    flip = np.eye(TILE, dtype=np.float32)[::-1]
    own = row_own.shape[1:]
    return pl.pallas_call(
        correlate_kernel,
        in_specs=[pl.BlockSpec(memory_space=pltpu.VMEM)] * 4,
        out_specs=pl.BlockSpec(memory_space=pl.ANY),
        out_shape=jax.ShapeDtypeStruct((row_total, col_total, LAGS), jnp.bfloat16),
        scratch_shapes=[
            pltpu.VMEM((STEPS, col_count) + own, jnp.bfloat16),
            pltpu.VMEM((STEPS, row_count) + own, jnp.bfloat16),
            pltpu.VMEM((row_total, 2 * SEGS, PAIR), jnp.float32),
            pltpu.VMEM((PAIR // F2, col_total * 2 * SEGS, F2), jnp.float32),
            pltpu.VMEM((2 * SEGS, col_total, PAIR), jnp.bfloat16),
            pltpu.VMEM((2, 2, pairs, PAIR), jnp.bfloat16),
            pltpu.VMEM((TILES, pairs, TILE), jnp.float32),
            pltpu.VMEM((row_total, col_total, LAGS), jnp.bfloat16),
            pltpu.SemaphoreType.DMA((2, 2 * (row_count - 1) + col_count - 1, STEPS)),
            pltpu.SemaphoreType.DMA((LAGS // TILE,)),
        ],
        compiler_params=pltpu.CompilerParams(
            vmem_limit_bytes=58 << 20, collective_id=1, has_side_effects=True
        ),
    )(row_own, col_own, tables, jnp.asarray(flip, jnp.bfloat16))


def local(strain, file_channels, file_counts, window_start):
    row_count = lax.axis_size("row")
    col_count = lax.axis_size("col")
    my_row = lax.axis_index("row")
    my_col = lax.axis_index("col")
    slot_total = strain.shape[0]
    window = lax.dynamic_slice_in_dim(strain, window_start[0], SEGS * NT, 1)
    slot_index = jnp.arange(slot_total, dtype=jnp.int32)
    live_slot = slot_index < file_counts[0]
    owner_row = file_channels // CH_DEV // col_count
    local_slot = file_channels % CH_DEV
    same_owner = (owner_row[:, None] == owner_row[None, :]) & live_slot[None, :]
    earlier = slot_index[None, :] < slot_index[:, None]
    position = jnp.sum((same_owner & earlier).astype(jnp.int32), axis=1)
    target = owner_row * CAP + position
    routing = (
        jnp.arange(row_count * CAP, dtype=jnp.int32)[:, None] == target[None, :]
    ) & live_slot[None, :]
    outgoing = jnp.dot(
        routing.astype(jnp.bfloat16), window, preferred_element_type=jnp.float32
    ).astype(jnp.bfloat16)
    labels = jnp.sum(jnp.where(routing, local_slot[None, :] + 1, 0), axis=1) - 1
    tail = jnp.broadcast_to(
        labels.astype(jnp.bfloat16)[:, None, None], (row_count * CAP, SEGS, 128)
    )
    outgoing = jnp.concatenate([outgoing.reshape(row_count * CAP, SEGS, NT), tail], axis=2)
    row_own, col_own, tables = spectra_of(outgoing.reshape(row_count, CAP, SEGS, NT + 128))
    return correlate(row_own, col_own, tables)


def solution(mesh):
    placed = (P(("row", "col"), None), P(("row", "col")), P(("row", "col")), P(("row", "col")))
    return jax.shard_map(
        local, mesh=mesh, in_specs=placed, out_specs=P("row", "col", None), check_vma=False
    )
```

```python
import functools
import math

import jax
import jax.numpy as jnp
import numpy as np
from jax import lax
from jax.experimental import pallas as pl
from jax.experimental.pallas import tpu as pltpu
from jax.sharding import PartitionSpec as P

NF = 2048
NT = 4096
LAGS = 1024
SEGS = 8
CH_DEV = 4
CAP = 2
SMOOTH = 32
EDGE = 128
N1 = 16
N2 = NT // N1
F2 = NF // N1
HALF = LAGS // 2
PAIR = 2 * F2
STEPS = NF // PAIR
TILE = 256
TILES = 2 * HALF // TILE
GROUP = 2
MESH = pl.DeviceIdType.MESH


def forward_tables():
    n2 = np.arange(N2)
    f1 = np.arange(N1)
    f2 = np.arange(F2)
    angle = 2 * np.pi * (np.outer(f1, n2) % NT) / NT
    twiddle = np.stack([np.cos(angle), -np.sin(angle)]).astype(np.float32)
    angle = 2 * np.pi * (np.outer(n2, f2) % N2) / N2
    c, s = np.cos(angle), np.sin(angle)
    second = np.block([[c, -s], [s, c]]).astype(np.float32)
    high = second.astype(jnp.bfloat16)
    low = (second - high.astype(np.float32)).astype(jnp.bfloat16)
    f = f1[:, None] + N1 * f2[None, :]
    distance = np.minimum(f + 0.5, NF - f - 0.5)
    taper = np.sin(0.5 * np.pi * np.minimum(distance / EDGE, 1.0)) ** 2
    turn = np.pi * f / NT
    shape = np.stack([taper, np.cos(turn), -np.sin(turn)]).astype(np.float32)
    return twiddle, high, low, shape


def lag_tables():
    m2 = 2 * np.arange(HALF) + 1
    f1 = np.arange(N1)
    f2 = N1 * np.arange(F2)
    a = np.pi * (np.outer(f1, m2) % (2 * NT)) / NT
    b = np.pi * (np.outer(f2, m2) % (2 * NT)) / NT
    first = np.stack([np.cos(a), np.sin(a)]).astype(np.float32)
    second = np.stack([np.cos(b), np.sin(b)]).astype(np.float32)
    return first, second


def shifted(value, lanes, amount):
    rolled = pltpu.roll(value, amount % F2, 1)
    source = lanes - amount
    return jnp.where((source >= 0) & (source < F2), rolled, 0.0)


def greet(axes):
    barrier = pltpu.get_barrier_semaphore()
    count = 0
    for axis in axes:
        size, me = lax.axis_size(axis), lax.axis_index(axis)
        for d in range(1, size):
            pl.semaphore_signal(barrier, inc=1, device_id={axis: lax.rem(me + d, size)}, device_id_type=MESH)
            count += 1
    pl.semaphore_wait(barrier, count)


def spectra_kernel(out_ref, *refs):
    sources, rest = refs[:6], refs[6:]
    row_ref, col_ref, w_ref = rest[:3]
    tw_ref, hi_ref, lo_ref, shape_ref, first_ref, second_ref = consts = rest[3:9]
    got, x_ref, z_ref, send_sem, recv_sem, const_sem = rest[9:]
    loads = [pltpu.make_async_copy(f, t, const_sem.at[k]) for k, (f, t) in enumerate(zip(sources, consts))]
    for load in loads[::-1]:
        load.start()
    size, me = lax.axis_size("row"), lax.axis_index("row")
    greet(("row",))

    def copy_of(d):
        peer = lax.rem(me + d, size)
        return pltpu.make_async_remote_copy(
            src_ref=out_ref.at[peer],
            dst_ref=got.at[d],
            send_sem=send_sem.at[d],
            recv_sem=recv_sem.at[d],
            device_id={"row": peer},
            device_id_type=MESH,
        )

    copies = [copy_of(d) for d in range(1, size)]
    for copy in copies:
        copy.start()
    got[0] = out_ref[me]
    for load in loads:
        load.wait()
    for k in range(HALF // TILE):
        lane = slice(k * TILE, (k + 1) * TILE)
        bc, bs = second_ref[0, :, lane], second_ref[1, :, lane]
        for f1 in range(N1):
            ac, as_ = first_ref[0, f1 : f1 + 1, lane], first_ref[1, f1 : f1 + 1, lane]
            t, at = f1 * F2 // PAIR, slice(f1 * F2 % PAIR, f1 * F2 % PAIR + F2)
            w_ref[t, k, at, :] = (ac * bc - as_ * bs).astype(jnp.bfloat16)
            w_ref[t, HALF // TILE + k, at, :] = (-(as_ * bc + ac * bs)).astype(jnp.bfloat16)
    for copy in copies:
        copy.wait()
    rows = x_ref.shape[0]
    slots = [(d, k) for d in range(size) for k in range(CAP)]
    label = [got[d, k, :, NT:].astype(jnp.float32) for d, k in slots]
    for ch in range(rows // SEGS):
        chosen = [v == np.float32(ch) for v in label]
        for h in range(0, NT, 128):
            total = None
            for (d, k), mask in zip(slots, chosen):
                term = jnp.where(mask, got[d, k, :, h : h + 128].astype(jnp.float32), 0.0)
                total = term if total is None else total + term
            x_ref[ch * SEGS : (ch + 1) * SEGS, h : h + 128] = total
    cosines = np.cos(2 * np.pi * np.arange(N1) / N1)
    sines = np.sin(2 * np.pi * np.arange(N1) / N1)

    def combine(values, weights):
        total = None
        for v, w in zip(values, weights):
            if abs(w) < 1e-9:
                continue
            term = v if abs(w - 1) < 1e-9 else (-v if abs(w + 1) < 1e-9 else v * np.float32(w))
            total = term if total is None else total + term
        return total

    for h in range(0, N2, 128):
        xs = [x_ref[:, k * N2 + h : k * N2 + h + 128] for k in range(N1)]
        even = [xs[k] + xs[k + N1 // 2] for k in range(N1 // 2)]
        odd = [xs[k] - xs[k + N1 // 2] for k in range(N1 // 2)]
        for f in range(N1 // 2 + 1):
            src = even if f % 2 == 0 else odd
            re = combine(src, [cosines[f * k % N1] for k in range(N1 // 2)])
            im = combine(src, [-sines[f * k % N1] for k in range(N1 // 2)])
            for f1, sign in {f: 1.0, (N1 - f) % N1: -1.0}.items() if f not in (0, N1 // 2) else ((f, 1.0),):
                tc = tw_ref[0, f1 : f1 + 1, h : h + 128]
                ts = tw_ref[1, f1 : f1 + 1, h : h + 128]
                if im is None:
                    zr, zi = re * tc, re * ts
                else:
                    i = im if sign > 0 else -im
                    zr, zi = re * tc - i * ts, re * ts + i * tc
                z_ref[f1 * rows : (f1 + 1) * rows, h : h + 128] = zr
                z_ref[f1 * rows : (f1 + 1) * rows, N2 + h : N2 + h + 128] = zi
    z = z_ref[...]
    zh = z.astype(jnp.bfloat16)
    zl = (z - zh.astype(jnp.float32)).astype(jnp.bfloat16)
    dot = functools.partial(jnp.dot, preferred_element_type=jnp.float32)
    z_ref[:, : 2 * F2] = dot(zh, hi_ref[...]) + dot(zl, hi_ref[...]) + dot(zh, lo_ref[...])

    lanes = lax.broadcasted_iota(jnp.int32, (rows, F2), 1)
    part = lambda f1, c: z_ref[f1 * rows : (f1 + 1) * rows, c * F2 : (c + 1) * F2]
    power = []
    for f1 in range(N1):
        re, im = part(f1, 0), part(f1, 1)
        power.append(re * re + im * im)
    prefix, suffix = [power[0]], [power[-1]]
    for k in range(1, N1):
        prefix.append(prefix[-1] + power[k])
        suffix.append(suffix[-1] + power[N1 - 1 - k])
    suffix = suffix[::-1]
    total = prefix[-1]
    reach = SMOOTH // N1
    middle = total
    for k in range(1, reach):
        middle = middle + shifted(total, lanes, k) + shifted(total, lanes, -k)
    for f1 in range(N1):
        window = middle + shifted(suffix[f1], lanes, reach) + shifted(prefix[f1], lanes, -reach)
        scale = shape_ref[0, f1 : f1 + 1] * lax.rsqrt(window * (1.0 / (2 * SMOOTH + 1)) + 1e-06)
        re, im = part(f1, 0) * scale, part(f1, 1) * scale
        tc, ts = shape_ref[1, f1 : f1 + 1], shape_ref[2, f1 : f1 + 1]
        tr, ti = re * tc - im * ts, re * ts + im * tc
        for ch in range(rows // SEGS):
            own = slice(ch * SEGS, (ch + 1) * SEGS)
            t, at = f1 * F2 // PAIR, slice(f1 * F2 % PAIR, f1 * F2 % PAIR + F2)
            col_ref[t, ch, :, at] = jnp.concatenate([re[own], im[own]], axis=0).astype(jnp.bfloat16)
            row_ref[t, ch, :, at] = jnp.concatenate([tr[own], ti[own]], axis=0).astype(jnp.bfloat16)


def spectra_of(outgoing):
    size = outgoing.shape[0]
    consts = [jnp.asarray(t) for t in forward_tables() + lag_tables()]
    rows = CH_DEV * SEGS
    shape = jax.ShapeDtypeStruct((STEPS, CH_DEV, 2 * SEGS, PAIR), jnp.bfloat16)
    return pl.pallas_call(
        spectra_kernel,
        out_shape=(shape, shape, jax.ShapeDtypeStruct((STEPS, TILES, PAIR, TILE), jnp.bfloat16)),
        in_specs=[pl.BlockSpec(memory_space=pltpu.VMEM)] + [pl.BlockSpec(memory_space=pl.ANY)] * len(consts),
        out_specs=[pl.BlockSpec(memory_space=pltpu.VMEM)] * 3,
        scratch_shapes=[pltpu.VMEM(t.shape, t.dtype) for t in consts]
        + [
            pltpu.VMEM(outgoing.shape, jnp.bfloat16),
            pltpu.VMEM((rows, NT), jnp.float32),
            pltpu.VMEM((N1 * rows, 2 * N2), jnp.float32),
            pltpu.SemaphoreType.DMA((size,)),
            pltpu.SemaphoreType.DMA((size,)),
            pltpu.SemaphoreType.DMA((len(consts),)),
        ],
        compiler_params=pltpu.CompilerParams(
            vmem_limit_bytes=48 << 20, collective_id=0, has_side_effects=True
        ),
    )(outgoing, *consts)


def tree(terms):
    while len(terms) > 1:
        terms = [terms[k] + terms[k + 1] for k in range(0, len(terms), 2)]
    return terms[0]


def correlate_kernel(
    row_ref, col_ref, w_ref, flip_ref, out_hbm, row_all, col_all, a32, b32, b_ref, cross, acc, out_ref, sems, out_sem
):
    row_total = row_all.shape[1] * CH_DEV
    col_total = col_all.shape[1] * CH_DEV
    share = row_total // TILES
    greet(("row", "col"))
    plans = []
    base = 0
    for axis, own, gathered in (("row", col_ref, col_all), ("col", row_ref, row_all)):
        size, me = lax.axis_size(axis), lax.axis_index(axis)
        for d in range(1, size):
            plans.append((axis, own, gathered, lax.rem(me + d, size), lax.rem(me + size - d, size), me, base + d - 1))
        base += size - 1

    def copy_of(plan, t, arriving):
        axis, own, gathered, peer, source, me, k = plan
        return pltpu.make_async_remote_copy(
            src_ref=own.at[pl.ds(t * GROUP, GROUP)],
            dst_ref=gathered.at[t, source if arriving else me],
            send_sem=sems.at[0, k, t],
            recv_sem=sems.at[1, k, t],
            device_id={axis: peer},
            device_id_type=MESH,
        )

    @pl.loop(0, STEPS // GROUP)
    def _(t):
        for plan in plans:
            copy_of(plan, t, False).start()

    row_me, col_me = lax.axis_index("row"), lax.axis_index("col")

    @pl.loop(0, STEPS)
    def _(t):
        col_all[t // GROUP, row_me, lax.rem(t, GROUP)] = col_ref[t]
        row_all[t // GROUP, col_me, lax.rem(t, GROUP)] = row_ref[t]

    def arrive(t):
        @pl.when(lax.rem(t, GROUP) == 0)
        def _():
            for plan in plans:
                copy_of(plan, t // GROUP, True).wait_recv()

        a32[...] = row_all[t // GROUP, :, lax.rem(t, GROUP)].reshape(a32.shape).astype(jnp.float32)
        for h in range(PAIR // F2):
            b32[h] = col_all[t // GROUP, :, lax.rem(t, GROUP), :, :, h * F2 : (h + 1) * F2].reshape(b32.shape[1:]).astype(jnp.float32)
            for k in range(2 * SEGS):
                rows = b32[h, pl.ds(k, col_total, stride=2 * SEGS), :]
                b_ref[k, :, h * F2 : (h + 1) * F2] = rows.astype(jnp.bfloat16)

    def cross_rows(first, now):
        for k in range(share):
            g = first + k
            for h in range(0, PAIR, F2):
                lane = slice(h, h + F2)
                real, imag = [], []
                for s in range(SEGS):
                    ar = jnp.broadcast_to(a32[g, s : s + 1, lane], (col_total, F2)).astype(jnp.bfloat16)
                    ai = jnp.broadcast_to(a32[g, SEGS + s : SEGS + s + 1, lane], (col_total, F2)).astype(jnp.bfloat16)
                    br, bi = b_ref[s, :, lane], b_ref[SEGS + s, :, lane]
                    real.append(ar * br + ai * bi)
                    imag.append(ai * br - ar * bi)
                at = pl.ds(pl.multiple_of(g * col_total, 16), col_total)
                cross[now, 0, at, lane] = tree(real)
                cross[now, 1, at, lane] = tree(imag)

    def lag_tile(i, t):
        before = lax.rem(t + 1, 2)
        part = jnp.dot(cross[before, i // (TILES // 2)], w_ref[t - 1, i], preferred_element_type=jnp.float32)
        acc[i] = acc[i] + part

    acc[...] = jnp.zeros_like(acc)
    arrive(jnp.int32(0))

    @pl.loop(0, TILES)
    def _(i):
        cross_rows(i * share, 0)

    @pl.loop(1, STEPS)
    def _(t):
        arrive(t)

        @pl.loop(0, TILES)
        def _(i):
            lag_tile(i, t)
            cross_rows(i * share, lax.rem(t, 2))

    @pl.loop(0, TILES)
    def _(i):
        lag_tile(i, STEPS)

    pairs = row_total * col_total
    place = lax.broadcasted_iota(jnp.int32, (pairs, TILE), 0) - (col_me * col_total + row_me) * CH_DEV
    same = place == 0
    for ch in range(1, CH_DEV):
        same = same | (place == ch * (col_total + 1))
    keep = jnp.where(same, 0.0, np.float32(1.0 / math.sqrt(SEGS * NF)))
    half = TILES // 2
    leaving = []

    def leave(first):
        lane = pl.ds(first, TILE)
        copy = pltpu.make_async_copy(out_ref.at[:, lane], out_hbm.at[:, lane], out_sem.at[first // TILE])
        copy.start()
        leaving.append(copy)

    for k in range(half):
        up = (acc[k] + acc[half + k]) * keep
        down = (acc[k] - acc[half + k]) * keep
        out_ref[:, HALF + k * TILE : HALF + (k + 1) * TILE] = up.astype(jnp.bfloat16)
        leave(HALF + k * TILE)
        turned = jnp.dot(down.astype(jnp.bfloat16), flip_ref[...], preferred_element_type=jnp.float32)
        out_ref[:, HALF - (k + 1) * TILE : HALF - k * TILE] = turned.astype(jnp.bfloat16)
        leave(HALF - (k + 1) * TILE)
    for copy in leaving:
        copy.wait()

    @pl.loop(0, STEPS // GROUP)
    def _(t):
        for plan in plans:
            copy_of(plan, t, False).wait_send()


def correlate(row_own, col_own, tables):
    row_count, col_count = lax.axis_size("row"), lax.axis_size("col")
    row_total, col_total = col_count * CH_DEV, row_count * CH_DEV
    pairs = row_total * col_total
    flip = np.eye(TILE, dtype=np.float32)[::-1]
    own = row_own.shape[1:]
    return pl.pallas_call(
        correlate_kernel,
        in_specs=[pl.BlockSpec(memory_space=pltpu.VMEM)] * 4,
        out_specs=pl.BlockSpec(memory_space=pl.ANY),
        out_shape=jax.ShapeDtypeStruct((pairs, LAGS), jnp.bfloat16),
        scratch_shapes=[
            pltpu.VMEM((STEPS // GROUP, col_count, GROUP) + own, jnp.bfloat16),
            pltpu.VMEM((STEPS // GROUP, row_count, GROUP) + own, jnp.bfloat16),
            pltpu.VMEM((row_total, 2 * SEGS, PAIR), jnp.float32),
            pltpu.VMEM((PAIR // F2, col_total * 2 * SEGS, F2), jnp.float32),
            pltpu.VMEM((2 * SEGS, col_total, PAIR), jnp.bfloat16),
            pltpu.VMEM((2, 2, pairs, PAIR), jnp.bfloat16),
            pltpu.VMEM((TILES, pairs, TILE), jnp.float32),
            pltpu.VMEM((pairs, LAGS), jnp.bfloat16),
            pltpu.SemaphoreType.DMA((2, row_count + col_count - 2, STEPS // GROUP)),
            pltpu.SemaphoreType.DMA((LAGS // TILE,)),
        ],
        compiler_params=pltpu.CompilerParams(
            vmem_limit_bytes=58 << 20, collective_id=1, has_side_effects=True
        ),
    )(row_own, col_own, tables, jnp.asarray(flip, jnp.bfloat16))


def local(strain, file_channels, file_counts, window_start):
    row_count = lax.axis_size("row")
    col_count = lax.axis_size("col")
    my_row = lax.axis_index("row")
    my_col = lax.axis_index("col")
    slot_total = strain.shape[0]
    window = lax.dynamic_slice_in_dim(strain, window_start[0], SEGS * NT, 1)
    slot_index = jnp.arange(slot_total, dtype=jnp.int32)
    live_slot = slot_index < file_counts[0]
    owner_row = file_channels // CH_DEV // col_count
    local_slot = file_channels % CH_DEV
    same_owner = (owner_row[:, None] == owner_row[None, :]) & live_slot[None, :]
    earlier = slot_index[None, :] < slot_index[:, None]
    position = jnp.sum((same_owner & earlier).astype(jnp.int32), axis=1)
    target = owner_row * CAP + position
    routing = (
        jnp.arange(row_count * CAP, dtype=jnp.int32)[:, None] == target[None, :]
    ) & live_slot[None, :]
    outgoing = jnp.dot(
        routing.astype(jnp.bfloat16), window, preferred_element_type=jnp.float32
    ).astype(jnp.bfloat16)
    labels = jnp.sum(jnp.where(routing, local_slot[None, :] + 1, 0), axis=1) - 1
    tail = jnp.broadcast_to(
        labels.astype(jnp.bfloat16)[:, None, None], (row_count * CAP, SEGS, 128)
    )
    outgoing = jnp.concatenate([outgoing.reshape(row_count * CAP, SEGS, NT), tail], axis=2)
    row_own, col_own, tables = spectra_of(outgoing.reshape(row_count, CAP, SEGS, NT + 128))
    row_total = CH_DEV * col_count
    col_total = CH_DEV * row_count
    lagged = correlate(row_own, col_own, tables)
    return lagged.reshape(row_total, col_total, LAGS)


def solution(mesh):
    placed = (P(("row", "col"), None), P(("row", "col")), P(("row", "col")), P(("row", "col")))
    return jax.shard_map(
        local, mesh=mesh, in_specs=placed, out_specs=P("row", "col", None), check_vma=False
    )
```
